256 devices in a mesh: seq: 16 (over y, z_hi, core), mp: 16 (over z_lo, x).
Axes of the slice: x: 4, y: 4, z: 8 (z_hi: 2, z_lo: 4; z = z_hi * 4 + z_lo), core: 2. Of those that a mesh axis runs over, the one named last changes fastest.
Arguments:
- hidden_in: bfloat16 [2048, 2048], P('seq'), may hold values from -0.59765625 to 0.59765625
- input_gain: float32 [2048], replicated, may hold values from 0.25 to 1.75
- w_query: bfloat16 [2048, 2048], P(None, 'mp'), may hold values from -0.125 to 0.125
- key_value_weight: bfloat16 [2048, 4096], P(None, 'mp'), may hold values from -1 to 1, as said below
- query_gain: float32 [128], replicated, may hold values from 0.25 to 1.75
- key_gain: float32 [128], replicated, may hold values from 0.25 to 1.75
- w_out: bfloat16 [2048, 2048], P('mp'), may hold values from -0.125 to 0.125
- post_gain: float32 [2048], replicated, may hold values from 0.25 to 1.75
- w_gate: bfloat16 [2048, 6144], P(None, 'mp'), may hold values from -0.125 to 0.125
- w_up: bfloat16 [2048, 6144], P(None, 'mp'), may hold values from -0.125 to 0.125
- w_down: bfloat16 [6144, 2048], P('mp'), may hold values from -0.078125 to 0.078125
- prefix_slot_cache: bfloat16 [32, 256, 8, 256], P('seq'), may hold values from -240 to 240, as said below
- block_table: int32 [32], replicated, may hold values from 0 to 31, each once
- request_prefix: int32 [32], replicated, may hold values from 0 to 3
- suffix_lengths: int32 [32], replicated, may hold values from 1 to 256, 2048 in all
Outputs:
- hidden_out: bfloat16 [2048, 2048], P('seq', 'mp')
- suffix_key_values: bfloat16 [2048, 2048], P('seq', 'mp')
The draws below stay inside these ranges and needn't reach their ends.
Inputs may be any that keep to these rules, and one draw needn't show every extreme that they name: block_table[p * 8 + i] is the slot holding block i of prefix p; every slot appears once. `suffix_lengths`: the lengths add up to 2048 and the longest is exactly 256. `prefix_slot_cache`: per slot, position and key-value head: a key in the first 128 entries, a value in the last 128. `key_value_weight`: columns of key-value head k: 2 equal blocks of 256, starting at k * 2 * 2 * 128.
All inputs are finite; a program needn't handle non-finite values.
Results may differ from the reference program's by a relative error of at most 0.025.
The reference program's roundings to bfloat16 on the way count: a program that leaves them out, or rounds other values in their place, can miss the bound.
Values may be sent and summed in bfloat16 or wider, within the bound.
A program may use at most 64 MiB of HBM per device.

```python
import math
import jax
import jax.numpy as jnp
import numpy as np
from jax import lax

MODEL_WIDTH = 2048
QUERY_HEADS = 16
KEY_VALUE_HEADS = 8
HEAD_WIDTH = 128
FF = 6144
SEQUENCE_TOKENS = 128
BLK_DEV = 2
SLOT_POSITIONS = 256
N_PREFIX = 4
REPLICAS = 2
SUFFIX_TOKENS = 2048
CACHE_SLOTS = 32
BPP = 8
PREF = 2048
REQUESTS = 32
MOST = 256


def draw_prefix_slot_cache(key, part):
    first_key = jax.random.fold_in(key, 0)
    sampled_values = jnp.clip(jax.random.normal(first_key, (CACHE_SLOTS, SLOT_POSITIONS, KEY_VALUE_HEADS, 2 * HEAD_WIDTH), jnp.float32), -6.0, 6.0)
    return sampled_values.astype(jnp.bfloat16)


def draw_key_value_weight(key, part):
    base_key = jax.random.fold_in(key, 17)
    sampled_values = jnp.clip(jax.random.normal(base_key, (MODEL_WIDTH, KEY_VALUE_HEADS, 1, 2 * HEAD_WIDTH), jnp.float32), -6.0, 6.0)
    sampled_values = sampled_values * MODEL_WIDTH ** (-0.5)
    copies = jnp.broadcast_to(sampled_values, (MODEL_WIDTH, KEY_VALUE_HEADS, REPLICAS, 2 * HEAD_WIDTH))
    return copies.reshape(MODEL_WIDTH, REPLICAS * 2 * KEY_VALUE_HEADS * HEAD_WIDTH).astype(jnp.bfloat16)


def plant(values, stream_key, smallest, top_value):
    place = [jax.random.randint(jax.random.fold_in(stream_key, axis), (), 0, length) for axis, length in enumerate(values.shape)]
    widest = values.shape.index(max(values.shape))
    next_to = place[:widest] + [(place[widest] + 1) % values.shape[widest]] + place[widest + 1:]
    return values.at[tuple(place)].set(smallest).at[tuple(next_to)].set(top_value)


def levels(stream_key, dims, pieces, smallest, top_value):
    factor_of, own = 1.0, jax.random.fold_in(stream_key, 6)
    for dim, parts in pieces:
        steps = jnp.exp(jax.random.uniform(jax.random.fold_in(own, dim), (parts,), jnp.float32, smallest / len(pieces), top_value / len(pieces)))
        factor_of = factor_of * jnp.repeat(steps, dims[dim] // parts).reshape([-1 if axis == dim else 1 for axis in range(len(dims))])
    return factor_of


def cumulative_ranks(count, slope):
    weights = [(1 << 20) // math.isqrt(grade ** slope) + 1 for grade in range(1, count + 1)]
    spread = 1 + sum(weights) // (1 << 30)
    return np.cumsum(np.array([max(1, weight // spread) for weight in weights]))


def ranked(own_key, dims, count, skew):
    table = cumulative_ranks(count, skew)
    ticket = jax.random.randint(jax.random.fold_in(own_key, 1), dims, 0, int(table[count - 1]))
    rank = jnp.searchsorted(jnp.asarray(table, jnp.int32), ticket, side="right")
    return jax.random.permutation(jax.random.fold_in(own_key, 2), count)[rank].astype(jnp.int32)


def profile(count, total, limit, slope):
    portions = [(1 << 20) // math.isqrt(rank ** slope) + 1 for rank in range(2, count + 1)]
    rest, holding = total - limit - (count - 1), [1] * (count - 1)
    while rest > 0:
        candidates = [i for i in range(count - 1) if holding[i] < limit]
        whole, remaining = sum([portions[i] for i in candidates]), rest
        for i in candidates:
            extra = min(limit - holding[i], max(1, remaining * portions[i] // whole), rest)
            holding[i] = holding[i] + extra
            rest = rest - extra
    return np.array([limit] + holding)


def ragged_sizes(own_key, count, total, bound, slope):
    if count == 2:
        one = jax.random.randint(own_key, (), max(1, total - bound), min(bound, total - 1) + 1)
        return jnp.stack([one, total - one])
    lengths = jnp.asarray(profile(count, total, bound, slope), jnp.int32)
    pairs = (count - 1) // 2
    giver, taker = lengths[1:1 + 2 * pairs:2], lengths[2:2 + 2 * pairs:2]
    slack = jnp.minimum(giver - 1, bound - taker)
    moved = jax.random.randint(jax.random.fold_in(own_key, 1), (pairs,), 0, 1 << 20) % (slack + 1)
    lengths = lengths.at[1:1 + 2 * pairs:2].set(giver - moved).at[2:2 + 2 * pairs:2].set(taker + moved)
    return lengths[jax.random.permutation(jax.random.fold_in(own_key, 2), count)]


def gaussian(key, shape, spread, most, shards=(), kind=jnp.bfloat16):
    level = levels(key, shape, shards, -0.22, 0.18) if shards else 1.0
    entries = jax.random.normal(key, shape, jnp.float32) * spread * level
    return jnp.minimum(jnp.maximum(entries, -most), most).astype(kind)


def setup_inputs(seed: int = 0) -> dict:
    seeds = jax.random.split(jax.random.key(seed), 16)
    hidden_in = gaussian(seeds[0], (SUFFIX_TOKENS, MODEL_WIDTH), 0.1, 0.59765625, ((0, 16),))
    input_gain = jnp.clip(1.0 + 0.15 * jax.random.normal(seeds[1], (MODEL_WIDTH,), jnp.float32), 0.25, 1.75)
    w_query = gaussian(seeds[2], (MODEL_WIDTH, QUERY_HEADS * HEAD_WIDTH), MODEL_WIDTH ** -0.5, 0.125, ((1, 16),))
    key_value_weight = draw_key_value_weight(jax.random.fold_in(seeds[15], 71), 0)
    query_gain = jnp.clip(1.0 + 0.15 * jax.random.normal(seeds[4], (HEAD_WIDTH,), jnp.float32), 0.25, 1.75)
    key_gain = jnp.clip(1.0 + 0.15 * jax.random.normal(seeds[5], (HEAD_WIDTH,), jnp.float32), 0.25, 1.75)
    w_out = gaussian(seeds[6], (QUERY_HEADS * HEAD_WIDTH, MODEL_WIDTH), (QUERY_HEADS * HEAD_WIDTH) ** -0.5, 0.125, ((0, 16),))
    post_gain = jnp.clip(1.0 + 0.15 * jax.random.normal(seeds[7], (MODEL_WIDTH,), jnp.float32), 0.25, 1.75)
    w_gate = gaussian(seeds[8], (MODEL_WIDTH, FF), MODEL_WIDTH ** -0.5, 0.125, ((1, 16),))
    w_up = gaussian(seeds[9], (MODEL_WIDTH, FF), MODEL_WIDTH ** -0.5, 0.125, ((1, 16),))
    w_down = gaussian(seeds[10], (FF, MODEL_WIDTH), FF ** -0.5, 0.078125, ((0, 16),))
    prefix_slot_cache = draw_prefix_slot_cache(jax.random.fold_in(seeds[15], 71), 0)
    block_table = jax.random.permutation(seeds[12], CACHE_SLOTS).astype(jnp.int32)
    request_prefix = plant(ranked(seeds[13], (REQUESTS,), N_PREFIX, 2), jax.random.fold_in(seeds[13], 3), 0, N_PREFIX - 1).astype(jnp.int32)
    suffix_lengths = ragged_sizes(seeds[14], REQUESTS, SUFFIX_TOKENS, MOST, 2).astype(jnp.int32)
    return dict(hidden_in=hidden_in, input_gain=input_gain, w_query=w_query, key_value_weight=key_value_weight, query_gain=query_gain, key_gain=key_gain, w_out=w_out, post_gain=post_gain, w_gate=w_gate, w_up=w_up, w_down=w_down, prefix_slot_cache=prefix_slot_cache, block_table=block_table, request_prefix=request_prefix, suffix_lengths=suffix_lengths)


EPSILON = 1e-06
THETA = 1000000.0
NEGATIVE_FLOOR = -1e+30

def token_tables(request_prefix, suffix_lengths, positions, prefix_length):
    request_ends = jnp.cumsum(suffix_lengths).astype(jnp.int32)
    starts = (request_ends - suffix_lengths).astype(jnp.int32)
    inside = ((positions[:, None] >= starts[None, :]) & (positions[:, None] < request_ends[None, :])).astype(jnp.int32)
    request_ids = jnp.arange(suffix_lengths.shape[0], dtype=jnp.int32)
    request_of = lax.optimization_barrier(jnp.sum(inside * request_ids[None, :], axis=1)).astype(jnp.int32)
    start_of = lax.optimization_barrier(jnp.sum(inside * starts[None, :], axis=1)).astype(jnp.int32)
    prefix_of = lax.optimization_barrier(jnp.sum(inside * request_prefix[None, :], axis=1)).astype(jnp.int32)
    rotary_pos = (prefix_length + positions - start_of).astype(jnp.int32)
    return (request_of, prefix_of, rotary_pos)

def row_norm(values, gain):
    return values * lax.rsqrt(lax.optimization_barrier(jnp.mean(values * values, axis=-1, keepdims=True)) + EPSILON) * gain

def head_norm(values, gain):
    return values * lax.rsqrt(lax.optimization_barrier(jnp.mean(values * values, axis=-1, keepdims=True)) + EPSILON) * gain

def rotate(values, rotary_pos):
    half_dim = values.shape[-1] // 2
    freq_ids = jnp.arange(half_dim).astype(jnp.float32)
    inverse = jnp.exp(freq_ids * (-2.0 * math.log(THETA) / values.shape[-1]))
    angles = rotary_pos.astype(jnp.float32)[:, None] * inverse[None, :]
    cosine = jnp.cos(angles)[:, None, :]
    sine_part = jnp.sin(angles)[:, None, :]
    first_half = values[..., :half_dim]
    second_half = values[..., half_dim:]
    return jnp.concatenate([first_half * cosine - second_half * sine_part, second_half * cosine + first_half * sine_part], axis=-1)

def allowed_keys(query_req, query_pre, query_pos, key_pre, key_req, key_pos):
    same_prefix = key_pre[None, :] == query_pre[:, None]
    same_request = (key_req[None, :] == query_req[:, None]) & (key_pos[None, :] <= query_pos[:, None])
    return same_prefix | same_request

def group_partial(query_rows_all, allowed, key_row_block, value_row_block):
    scaling = 1.0 / math.sqrt(query_rows_all.shape[-1])
    scores = jnp.einsum('nkgd,mkd->nkgm', query_rows_all.astype(jnp.float32), key_row_block.astype(jnp.float32)) * scaling
    allowed_full = allowed[:, None, None, :]
    scores = jnp.where(allowed_full, scores, NEGATIVE_FLOOR)
    highest_score = lax.optimization_barrier(jnp.max(scores, axis=-1))
    weights = jnp.where(allowed_full, jnp.exp(scores - highest_score[..., None]), 0.0)
    total_weight = lax.optimization_barrier(jnp.sum(weights, axis=-1))
    rounded = lax.optimization_barrier(weights.astype(jnp.bfloat16)).astype(jnp.float32)
    summed = jnp.einsum('nkgm,mkd->nkgd', rounded, value_row_block.astype(jnp.float32))
    layer_output = (summed / jnp.maximum(total_weight, 1.0)[..., None]).astype(jnp.bfloat16)
    return (highest_score, total_weight, layer_output)

def merge_group(running, highest_score, total_weight, layer_output):
    best_score, weight_sum, accumulated = running
    new_best = jnp.maximum(best_score, highest_score)
    old_factor = jnp.exp(best_score - new_best)
    new_factor = total_weight * jnp.exp(highest_score - new_best)
    return (new_best, weight_sum * old_factor + new_factor, accumulated * old_factor[..., None] + new_factor[..., None] * layer_output.astype(jnp.float32))

def reference(hidden_in, input_gain, w_query, key_value_weight, query_gain, key_gain, w_out, post_gain, w_gate, w_up, w_down, prefix_slot_cache, block_table, request_prefix, suffix_lengths):
    group_width = QUERY_HEADS // KEY_VALUE_HEADS
    hidden_f32 = hidden_in.astype(jnp.float32)
    normed = row_norm(hidden_f32, input_gain).astype(jnp.bfloat16)
    positions = jnp.arange(SUFFIX_TOKENS, dtype=jnp.int32)
    request_of, prefix_of, rotary_pos = token_tables(request_prefix, suffix_lengths, positions, PREF)
    query_raw = jnp.dot(normed, w_query, preferred_element_type=jnp.float32).reshape(SUFFIX_TOKENS, QUERY_HEADS, HEAD_WIDTH)
    query_rows_all = rotate(head_norm(query_raw, query_gain), rotary_pos).astype(jnp.bfloat16)
    query_rows_all = query_rows_all.reshape(SUFFIX_TOKENS, KEY_VALUE_HEADS, group_width, HEAD_WIDTH)
    first_copy = key_value_weight.reshape(MODEL_WIDTH, KEY_VALUE_HEADS, REPLICAS, 2 * HEAD_WIDTH)[:, :, 0, :].reshape(MODEL_WIDTH, 2 * KEY_VALUE_HEADS * HEAD_WIDTH)
    unscaled_pairs = jnp.dot(normed, first_copy, preferred_element_type=jnp.float32).astype(jnp.bfloat16)
    unscaled_pairs = unscaled_pairs.reshape(SUFFIX_TOKENS, KEY_VALUE_HEADS, 2, HEAD_WIDTH)
    key_row_block = rotate(head_norm(unscaled_pairs[:, :, 0].astype(jnp.float32), key_gain), rotary_pos).astype(jnp.bfloat16)
    value_row_block = unscaled_pairs[:, :, 1]
    suffix_key_values = jnp.stack([key_row_block, value_row_block], axis=2).reshape(SUFFIX_TOKENS, 2 * KEY_VALUE_HEADS * HEAD_WIDTH)
    slot_ids = jnp.arange(CACHE_SLOTS, dtype=jnp.int32)
    owner_hits = (block_table[:, None] == slot_ids[None, :]).astype(jnp.int32)
    slot_prefix = lax.optimization_barrier(jnp.sum(owner_hits * (slot_ids // BPP)[:, None], axis=0)).astype(jnp.int32)
    group_list = SUFFIX_TOKENS // SEQUENCE_TOKENS
    cache_extent = BLK_DEV * SLOT_POSITIONS
    grouped_cache = prefix_slot_cache.reshape(group_list, cache_extent, KEY_VALUE_HEADS, 2 * HEAD_WIDTH)
    grouped_keys = key_row_block.reshape(group_list, SEQUENCE_TOKENS, KEY_VALUE_HEADS, HEAD_WIDTH)
    grouped_values = value_row_block.reshape(group_list, SEQUENCE_TOKENS, KEY_VALUE_HEADS, HEAD_WIDTH)
    pre_groups = jnp.repeat(slot_prefix, SLOT_POSITIONS).reshape(group_list, cache_extent)
    req_groups = request_of.reshape(group_list, SEQUENCE_TOKENS)
    pos_groups = positions.reshape(group_list, SEQUENCE_TOKENS)
    tiled_queries = query_rows_all.reshape(group_list, SEQUENCE_TOKENS, KEY_VALUE_HEADS, group_width, HEAD_WIDTH)
    prefix_tiles = prefix_of.reshape(group_list, SEQUENCE_TOKENS)

    def one_group(running, members):
        cache_rows, group_keys, group_values, group_pre, group_req, group_pos = members
        all_keys = jnp.concatenate([cache_rows[..., :HEAD_WIDTH], group_keys], axis=0)
        all_values = jnp.concatenate([cache_rows[..., HEAD_WIDTH:], group_values], axis=0)
        key_pre = jnp.concatenate([group_pre, jnp.full((SEQUENCE_TOKENS,), -1, jnp.int32)])
        key_req = jnp.concatenate([jnp.full((cache_extent,), -1, jnp.int32), group_req])
        key_pos = jnp.concatenate([jnp.zeros((cache_extent,), jnp.int32), group_pos])

        def one_tile(tile_members):
            tile_queries, tile_req, tile_pre, tile_pos = tile_members
            allowed = allowed_keys(tile_req, tile_pre, tile_pos, key_pre, key_req, key_pos)
            return group_partial(tile_queries, allowed, all_keys, all_values)
        highest_score, total_weight, layer_output = lax.map(one_tile, (tiled_queries, req_groups, prefix_tiles, pos_groups))
        highest_score = highest_score.reshape(SUFFIX_TOKENS, KEY_VALUE_HEADS, group_width)
        total_weight = total_weight.reshape(SUFFIX_TOKENS, KEY_VALUE_HEADS, group_width)
        layer_output = layer_output.reshape(SUFFIX_TOKENS, KEY_VALUE_HEADS, group_width, HEAD_WIDTH)
        return (merge_group(running, highest_score, total_weight, layer_output), None)
    starting_carry = (jnp.full((SUFFIX_TOKENS, KEY_VALUE_HEADS, group_width), NEGATIVE_FLOOR, jnp.float32), jnp.zeros((SUFFIX_TOKENS, KEY_VALUE_HEADS, group_width), jnp.float32), jnp.zeros((SUFFIX_TOKENS, KEY_VALUE_HEADS, group_width, HEAD_WIDTH), jnp.float32))
    running, _ = lax.scan(one_group, starting_carry, (grouped_cache, grouped_keys, grouped_values, pre_groups, req_groups, pos_groups))
    best_score, weight_sum, accumulated = running
    attended = (accumulated / weight_sum[..., None]).astype(jnp.bfloat16).reshape(SUFFIX_TOKENS, QUERY_HEADS * HEAD_WIDTH)
    residual = (hidden_f32 + jnp.dot(attended, w_out, preferred_element_type=jnp.float32)).astype(jnp.bfloat16)
    post_normed = row_norm(residual.astype(jnp.float32), post_gain).astype(jnp.bfloat16)
    gate_terms = jnp.dot(post_normed, w_gate, preferred_element_type=jnp.float32)
    up_terms = jnp.dot(post_normed, w_up, preferred_element_type=jnp.float32)
    middle = (jax.nn.silu(gate_terms) * up_terms).astype(jnp.bfloat16)
    hidden_out = (residual.astype(jnp.float32) + jnp.dot(middle, w_down, preferred_element_type=jnp.float32)).astype(jnp.bfloat16)
    return (hidden_out, suffix_key_values)
```

```python
import math

import jax
import jax.numpy as jnp
from jax import lax
from jax.experimental import pallas as pl
from jax.experimental.pallas import tpu as pltpu
from jax.sharding import PartitionSpec as P

MESH = pl.DeviceIdType.MESH
HEAD = 128
TOK = 128
SEQ = 16
EPSILON = 1e-06
THETA = 1000000.0
FLOOR = -1e30
SCALE = math.log2(math.e) / math.sqrt(HEAD)
F32 = jnp.float32
BF16 = jnp.bfloat16


def dot(a, b, ca, cb):
    return lax.dot_general(a, b, (((ca,), (cb,)), ((), ())), preferred_element_type=F32)


def remote(src, dst, ss, rs, dev):
    return pltpu.make_async_remote_copy(
        src_ref=src, dst_ref=dst, send_sem=ss, recv_sem=rs, device_id=dev, device_id_type=MESH
    )


def row_scale(values):
    return lax.rsqrt(jnp.mean(values * values, axis=-1, keepdims=True) + EPSILON)


def slot_part(keys, values_t, queries, visible):
    scores = [dot(k, queries, 1, 1) for k in keys]
    peaks = [
        jnp.where(v, jnp.max(s, axis=0, keepdims=True) * SCALE, FLOOR)
        for s, v in zip(scores, visible)
    ]
    peak = jnp.maximum(peaks[0], peaks[1])
    total, out = None, None
    for s, v, vt in zip(scores, visible, values_t):
        weight = jnp.exp2(s * SCALE - jnp.where(v, peak, 1e30))
        part = jnp.sum(weight, axis=0, keepdims=True)
        prod = dot(vt, weight.astype(BF16), 1, 0)
        total = part if total is None else total + part
        out = prod if out is None else out + prod
    return peak, total, out


def kernel(
    table_ref,
    request_prefix_ref,
    lengths_ref,
    hidden_hbm,
    gain_hbm,
    post_gain_hbm,
    q_gain_ref,
    k_gain_ref,
    cos_ref,
    sin_ref,
    cache_ref,
    wq_hbm,
    wkv_hbm,
    wo_hbm,
    wg_hbm,
    wu_hbm,
    wd_hbm,
    out_ref,
    suffix_ref,
    hidden,
    gain,
    post_gain,
    wq,
    wkv,
    wo,
    wg,
    wu,
    wd,
    normed,
    peer_cache,
    vt,
    q_all,
    suf,
    half_out,
    half_stat,
    res_out,
    res_stat,
    back_out,
    back_stat,
    prefix_rows,
    part,
    part_x,
    part_z,
    sent_z,
    part2,
    part2_x,
    part2_z,
    sent2_z,
    gathered,
    dma_sem,
    kv_s,
    kv_r,
    suf_s,
    suf_r,
    q_s,
    q_r,
    o_s,
    o_r,
    st_s,
    st_r,
    x_s,
    x_r,
    z_s,
    z_r,
    x2_s,
    x2_r,
    z2_s,
    z2_r,
    g_s,
    g_r,
):
    s = lax.axis_index("seq")
    m = lax.axis_index("mp")
    y, zh, c = lax.div(s, 4), lax.rem(lax.div(s, 2), 2), lax.rem(s, 2)
    zl, x = lax.div(m, 4), lax.rem(m, 4)

    def at_seq(i):
        return {"seq": i}

    def at_mp(i):
        return {"mp": i}

    loads = []
    for k, (src, dst) in enumerate(
        [
            (hidden_hbm, hidden),
            (gain_hbm, gain),
            (wq_hbm, wq),
            (wkv_hbm, wkv),
            (wo_hbm, wo),
            (post_gain_hbm, post_gain),
            (wg_hbm, wg),
            (wu_hbm, wu),
            (wd_hbm, wd),
        ]
    ):
        copy = pltpu.make_async_copy(src, dst, dma_sem.at[k])
        copy.start()
        loads.append(copy)

    z_peer = at_seq(y * 4 + (1 - zh) * 2 + c)
    yc_peers = []
    for dy, dc in ((0, 1), (1, 0), (1, 1), (3, 0), (3, 1), (2, 0), (2, 1)):
        yy, cc = lax.rem(y + dy, 4), lax.rem(c + dc, 2)
        yc_peers.append((yy * 2 + cc, at_seq(yy * 4 + zh * 2 + cc)))
    mine = y * 2 + c
    after = [at_seq(lax.rem(s + 2, SEQ)), at_seq(lax.rem(s + 1, SEQ))]
    before = [at_seq(lax.rem(s + 14, SEQ)), at_seq(lax.rem(s + 15, SEQ))]
    hops = (2, 1, 3)
    x_peers = [at_mp(zl * 4 + lax.rem(x + i, 4)) for i in hops]
    z_peers = [at_mp(lax.rem(zl + i, 4) * 4 + x) for i in hops]

    barrier = pltpu.get_barrier_semaphore()
    everyone = [z_peer] + [p for _, p in yc_peers] + after + before + x_peers + z_peers
    for dev in everyone:
        pl.semaphore_signal(barrier, inc=1, device_id=dev, device_id_type=MESH)

    token = lax.broadcasted_iota(jnp.int32, (SEQ, TOK), 0) * TOK + lax.broadcasted_iota(
        jnp.int32, (SEQ, TOK), 1
    )
    own_token = s * TOK + lax.broadcasted_iota(jnp.int32, (1, TOK), 1)
    prefix = jnp.zeros((SEQ, TOK), jnp.int32)
    own_start = jnp.zeros((1, TOK), jnp.int32)
    begin = jnp.int32(0)
    for r in range(32):
        end = begin + lengths_ref[r]
        prefix = jnp.where((token >= begin) & (token < end), request_prefix_ref[r], prefix)
        own_start = jnp.where((own_token >= begin) & (own_token < end), begin, own_start)
        begin = end
    prefix_rows[...] = prefix

    slot_ids = [2 * s, 2 * s + 1, 2 * s + 4 - 8 * zh, 2 * s + 5 - 8 * zh]
    slot_prefix = [jnp.int32(0)] * 4
    for i in range(32):
        held = table_ref[i]
        slot_prefix = [
            jnp.where(held == slot, jnp.int32(i // 8), p) for slot, p in zip(slot_ids, slot_prefix)
        ]

    loads[0].wait()
    loads[1].wait()
    raw = hidden[...].astype(F32)
    normed[...] = (raw * row_scale(raw) * gain[...]).astype(BF16)

    pl.semaphore_wait(barrier, len(everyone))

    kv_copies = []
    for b in range(2):
        rows = pl.ds(b * 256, 256)
        copy = remote(cache_ref.at[rows], peer_cache.at[rows], kv_s.at[b], kv_r.at[b], z_peer)
        copy.start()
        kv_copies.append(copy)

    cosine, sine = cos_ref[...], sin_ref[...]

    def head_rope(values, g):
        scaled = values * row_scale(values) * g
        return (scaled * cosine + pltpu.roll(scaled, HEAD // 2, 1) * sine).astype(BF16)

    loads[2].wait()
    q_raw = dot(normed[...], wq[...], 1, 0)
    q_all[mine] = head_rope(q_raw, q_gain_ref[...])
    q_copies = []
    for k, (_, dev) in enumerate(yc_peers):
        copy = remote(q_all.at[mine], q_all.at[mine], q_s.at[k], q_r.at[mine], dev)
        copy.start()
        q_copies.append(copy)

    loads[3].wait()
    pair = dot(normed[...], wkv[...], 1, 0).astype(BF16)
    key_rows = head_rope(pair[:, :HEAD].astype(F32), k_gain_ref[...])
    value_rows = pair[:, HEAD:]
    suf[2, 0] = key_rows
    suf[2, 1] = value_rows.T
    suf_copies = []
    for k in range(2):
        copy = remote(suf.at[2], suf.at[k], suf_s.at[k], suf_r.at[k], after[k])
        copy.start()
        suf_copies.append(copy)
    suffix_ref[...] = jnp.where(lax.rem(m, 2) == 0, key_rows, value_rows)

    for b in range(2):
        vt[b] = cache_ref[pl.ds(b * 256, 256), pl.ds(HEAD, HEAD)].T

    def block_of(j):
        yy = lax.rem(y + lax.div(j, 2), 4)
        cc = lax.rem(c + lax.rem(j, 2), 2)
        return yy * 2 + cc, yy * 4 + zh * 2 + cc

    def attend(block, tokens, cache, first):
        queries = q_all[block]
        pre = prefix_rows[pl.ds(tokens, 1), :]
        return slot_part(
            [cache[pl.ds(b * 256, 256), pl.ds(0, HEAD)] for b in range(2)],
            [vt[first + b] for b in range(2)],
            queries,
            [pre == slot_prefix[first + b] for b in range(2)],
        )

    def first_half(j, carry):
        block, tokens = block_of(j)

        @pl.when(j > 0)
        def _():
            remote(q_all.at[block], q_all.at[block], q_s.at[0], q_r.at[block], z_peer).wait_recv()

        peak, total, out = attend(block, tokens, cache_ref, 0)
        half_stat[j, pl.ds(0, 1), :] = peak
        half_stat[j, pl.ds(1, 1), :] = total
        half_out[j] = out
        return carry

    lax.fori_loop(0, 8, first_half, 0)

    for copy in suf_copies:
        copy.wait_recv()
    queries = q_all[mine]
    suffix_scores = []
    for k in range(3):
        at = (s - 2 + k) * TOK + lax.broadcasted_iota(jnp.int32, (TOK, TOK), 0)
        seen = (at >= own_start) & (at <= own_token)
        suffix_scores.append(
            jnp.where(seen, dot(suf[k, 0], queries, 1, 1) * SCALE, FLOOR)
        )
    suffix_peak = jnp.max(
        jnp.maximum(jnp.maximum(suffix_scores[0], suffix_scores[1]), suffix_scores[2]),
        axis=0,
        keepdims=True,
    )
    suffix_total = jnp.zeros((1, TOK), F32)
    suffix_out = jnp.zeros((HEAD, TOK), F32)
    for k in range(3):
        weight = jnp.exp2(suffix_scores[k] - suffix_peak)
        suffix_total += jnp.sum(weight, axis=0, keepdims=True)
        suffix_out += dot(suf[k, 1], weight.astype(BF16), 1, 0)

    for copy in kv_copies:
        copy.wait_recv()
    for b in range(2):
        vt[2 + b] = peer_cache[pl.ds(b * 256, 256), pl.ds(HEAD, HEAD)].T

    def second_half(i, carry):
        j = 7 - i
        block, tokens = block_of(j)
        peak1, total1, out1 = attend(block, tokens, peer_cache, 2)
        peak0 = half_stat[j, pl.ds(0, 1), :]
        total0 = half_stat[j, pl.ds(1, 1), :]
        peak = jnp.maximum(peak0, peak1)
        f0, f1 = jnp.exp2(peak0 - peak), jnp.exp2(peak1 - peak)
        total = total0 * f0 + total1 * f1
        inverse = 1.0 / jnp.maximum(total, 1.0)
        res_out[block] = (half_out[j] * (f0 * inverse) + out1 * (f1 * inverse)).astype(BF16)
        res_stat[block, pl.ds(0, 1), :] = peak
        res_stat[block, pl.ds(1, 1), :] = total

        @pl.when(j > 0)
        def _():
            dev = at_seq(tokens)
            remote(
                res_out.at[block], back_out.at[mine], o_s.at[block], o_r.at[mine], dev
            ).start()
            remote(
                res_stat.at[block], back_stat.at[mine], st_s.at[block], st_r.at[mine], dev
            ).start()

        return carry

    lax.fori_loop(0, 8, second_half, 0)

    parts = [(suffix_peak, suffix_total, suffix_out / suffix_total)]
    parts.append((res_stat[mine, pl.ds(0, 1), :], res_stat[mine, pl.ds(1, 1), :], res_out[mine]))
    for block, dev in yc_peers:
        remote(res_out.at[block], back_out.at[block], o_s.at[block], o_r.at[block], dev).wait_recv()
        remote(
            res_stat.at[block], back_stat.at[block], st_s.at[block], st_r.at[block], dev
        ).wait_recv()
        parts.append(
            (back_stat[block, pl.ds(0, 1), :], back_stat[block, pl.ds(1, 1), :], back_out[block])
        )
    best = parts[0][0]
    for peak, _, _ in parts[1:]:
        best = jnp.maximum(best, peak)
    weight_sum, accumulated = None, None
    for peak, total, out in parts:
        factor = total * jnp.exp2(peak - best)
        term = factor * out.astype(F32)
        weight_sum = factor if weight_sum is None else weight_sum + factor
        accumulated = term if accumulated is None else accumulated + term
    attended = (accumulated / weight_sum).astype(BF16)
    attended = attended.T

    def reduce_scatter(left, weight, blocks, from_x, from_z, to_z, xs, xr, zs, zr):
        sends = []
        for i in (2, 1, 3, 0):
            zz = lax.rem(zl + i, 4)
            prod = dot(left, weight[:, pl.ds(pl.multiple_of(zz * 512, 512), 512)], 1, 0)
            prod = prod.astype(BF16)
            for k in range(4):
                blocks[i, k] = prod[:, k * HEAD : (k + 1) * HEAD]
            for k, hop in enumerate(hops):
                copy = remote(
                    blocks.at[i, lax.rem(x + hop, 4)],
                    from_x.at[i, k],
                    xs.at[i, k],
                    xr.at[i, k],
                    x_peers[k],
                )
                copy.start()
                sends.append(copy)
        z_sends = []
        for n, i in enumerate((2, 1, 3, 0)):
            for k in range(3):
                sends[n * 3 + k].wait_recv()
            acc = blocks[i, x].astype(F32)
            for k in range(3):
                acc = acc + from_x[i, k].astype(F32)
            if i:
                to_z[n] = acc.astype(BF16)
                copy = remote(to_z.at[n], from_z.at[n], zs.at[n], zr.at[n], z_peers[n])
                copy.start()
                z_sends.append(copy)
        for n, copy in enumerate(z_sends):
            copy.wait_recv()
            acc = acc + from_z[n].astype(F32)
        return acc, sends + z_sends

    loads[4].wait()
    summed, sends1 = reduce_scatter(
        attended, wo, part, part_x, part_z, sent_z, x_s, x_r, z_s, z_r
    )
    columns = pl.ds(pl.multiple_of(m * HEAD, HEAD), HEAD)
    residual = (hidden[:, columns].astype(F32) + summed).astype(BF16)

    gathered[m] = residual
    g_copies = []

    def share(block, dev):
        n = len(g_copies)
        copy = remote(gathered.at[block], gathered.at[block], g_s.at[n], g_r.at[block], dev)
        copy.start()
        g_copies.append(copy)

    def arrived(block):
        remote(
            gathered.at[block], gathered.at[block], g_s.at[0], g_r.at[block], z_peers[0]
        ).wait_recv()

    for dev in z_peers:
        share(m, dev)
    for dev in x_peers:
        share(m, dev)
    for i in (1, 3, 2):
        block = lax.rem(zl + i, 4) * 4 + x
        arrived(block)
        for dev in x_peers:
            share(block, dev)
    for i in (1, 3, 2):
        for zz in range(4):
            arrived(zz * 4 + lax.rem(x + i, 4))

    square = jnp.zeros((TOK, HEAD), F32)
    for k in range(16):
        v = gathered[k].astype(F32)
        square = square + v * v
    scale = lax.rsqrt(jnp.sum(square, axis=-1, keepdims=True) * (1.0 / 2048) + EPSILON)
    loads[5].wait()
    for k in range(16):
        cols = pl.ds(k * HEAD, HEAD)
        normed[:, cols] = (gathered[k].astype(F32) * scale * post_gain[:, cols]).astype(BF16)
    loads[6].wait()
    gate = dot(normed[...], wg[...], 1, 0)
    loads[7].wait()
    up = dot(normed[...], wu[...], 1, 0)
    middle = (gate / (1.0 + jnp.exp(-gate)) * up).astype(BF16)
    loads[8].wait()
    summed, sends2 = reduce_scatter(
        middle, wd, part2, part2_x, part2_z, sent2_z, x2_s, x2_r, z2_s, z2_r
    )
    out_ref[...] = (residual.astype(F32) + summed).astype(BF16)

    for copy in kv_copies + suf_copies + q_copies + sends1 + sends2 + g_copies:
        copy.wait_send()
    for block, dev in yc_peers:
        remote(res_out.at[block], back_out.at[block], o_s.at[block], o_r.at[block], dev).wait_send()
        remote(
            res_stat.at[block], back_stat.at[block], st_s.at[block], st_r.at[block], dev
        ).wait_send()


def local(
    hidden_in,
    input_gain,
    w_query,
    key_value_weight,
    query_gain,
    key_gain,
    w_out,
    post_gain,
    w_gate,
    w_up,
    w_down,
    prefix_slot_cache,
    block_table,
    request_prefix,
    suffix_lengths,
):
    my_seq = lax.axis_index("seq")
    my_model = lax.axis_index("mp")
    own = my_seq * TOK + jnp.arange(TOK, dtype=jnp.int32)
    ends = jnp.cumsum(suffix_lengths)
    starts = ends - suffix_lengths
    inside = (own[:, None] >= starts[None, :]) & (own[:, None] < ends[None, :])
    start_of = jnp.sum(inside.astype(jnp.int32) * starts[None, :], axis=1)
    rotary_pos = (2048 + own - start_of).astype(F32)
    half = HEAD // 2
    inverse = jnp.exp(jnp.arange(half).astype(F32) * (-2.0 * math.log(THETA) / HEAD))
    angles = rotary_pos[:, None] * inverse[None, :]
    cosine, sine = jnp.cos(angles), jnp.sin(angles)
    cosine = jnp.concatenate([cosine, cosine], axis=1)
    sine = jnp.concatenate([-sine, sine], axis=1)
    cache = lax.dynamic_slice_in_dim(prefix_slot_cache, my_model // 2, 1, 2).reshape(512, 2 * HEAD)

    vmem = pl.BlockSpec(memory_space=pltpu.VMEM)
    smem = pl.BlockSpec(memory_space=pltpu.SMEM)
    hbm = pl.BlockSpec(memory_space=pl.ANY)
    V = pltpu.VMEM
    D = pltpu.SemaphoreType.DMA
    block = (TOK, HEAD)
    return pl.pallas_call(
        kernel,
        out_shape=(
            jax.ShapeDtypeStruct((TOK, HEAD), BF16),
            jax.ShapeDtypeStruct((TOK, HEAD), BF16),
        ),
        in_specs=[smem] * 3 + [hbm] * 3 + [vmem] * 5 + [hbm] * 6,
        out_specs=(vmem, vmem),
        scratch_shapes=[
            V((128, 2048), BF16),
            V((1, 2048), F32),
            V((1, 2048), F32),
            V((2048, 128), BF16),
            V((2048, 256), BF16),
            V((128, 2048), BF16),
            V((2048, 384), BF16),
            V((2048, 384), BF16),
            V((384, 2048), BF16),
            V((128, 2048), BF16),
            V((512, 256), BF16),
            V((4, 128, 256), BF16),
            V((8,) + block, BF16),
            V((3, 2) + block, BF16),
            V((8,) + block, F32),
            V((8, 8, 128), F32),
            V((8,) + block, BF16),
            V((8, 8, 128), F32),
            V((8,) + block, BF16),
            V((8, 8, 128), F32),
            V((16, 128), jnp.int32),
            V((4, 4) + block, BF16),
            V((4, 3) + block, BF16),
            V((3,) + block, BF16),
            V((3,) + block, BF16),
            V((4, 4) + block, BF16),
            V((4, 3) + block, BF16),
            V((3,) + block, BF16),
            V((3,) + block, BF16),
            V((16,) + block, BF16),
            D((9,)),
            D((2,)),
            D((2,)),
            D((2,)),
            D((2,)),
            D((7,)),
            D((8,)),
            D((8,)),
            D((8,)),
            D((8,)),
            D((8,)),
            D((4, 3)),
            D((4, 3)),
            D((3,)),
            D((3,)),
            D((4, 3)),
            D((4, 3)),
            D((3,)),
            D((3,)),
            D((15,)),
            D((16,)),
        ],
        compiler_params=pltpu.CompilerParams(
            collective_id=0, has_side_effects=True, vmem_limit_bytes=48 * 1024 * 1024
        ),
        name="layer",
    )(
        block_table,
        request_prefix,
        suffix_lengths,
        hidden_in,
        input_gain.reshape(1, -1),
        post_gain.reshape(1, -1),
        query_gain.reshape(1, -1),
        key_gain.reshape(1, -1),
        cosine,
        sine,
        cache,
        w_query,
        key_value_weight,
        w_out,
        w_gate,
        w_up,
        w_down,
    )


def solution(mesh):
    in_specs = (
        P("seq", None),
        P(),
        P(None, "mp"),
        P(None, "mp"),
        P(),
        P(),
        P("mp", None),
        P(),
        P(None, "mp"),
        P(None, "mp"),
        P("mp", None),
        P("seq", None, None, None),
        P(),
        P(),
        P(),
    )
    out_specs = (P("seq", "mp"), P("seq", "mp"))
    return jax.shard_map(local, mesh=mesh, in_specs=in_specs, out_specs=out_specs, check_vma=False)
```

```python
import functools
import math

import jax
import jax.numpy as jnp
from jax import lax
from jax.experimental import pallas as pl
from jax.experimental.pallas import tpu as pltpu
from jax.sharding import PartitionSpec as P

MESH = pl.DeviceIdType.MESH
HEAD = 128
TOK = 128
SEQ = 16
EPSILON = 1e-06
THETA = 1000000.0
FLOOR = -1e30
SCALE = math.log2(math.e) / math.sqrt(HEAD)
F32 = jnp.float32
BF16 = jnp.bfloat16


def dot(a, b, ca, cb):
    return lax.dot_general(a, b, (((ca,), (cb,)), ((), ())), preferred_element_type=F32)


def remote(src, dst, ss, rs, dev):
    return pltpu.make_async_remote_copy(
        src_ref=src, dst_ref=dst, send_sem=ss, recv_sem=rs, device_id=dev, device_id_type=MESH
    )


def row_scale(values):
    return lax.rsqrt(jnp.mean(values * values, axis=-1, keepdims=True) + EPSILON)


def slot_part(keys, values_t, queries, visible):
    scores = [dot(k, queries, 1, 1) for k in keys]
    peaks = [
        jnp.where(v, jnp.max(s, axis=0, keepdims=True) * SCALE, FLOOR)
        for s, v in zip(scores, visible)
    ]
    peak = jnp.maximum(peaks[0], peaks[1])
    total, out = None, None
    for s, v, vt in zip(scores, visible, values_t):
        weight = jnp.exp2(s * SCALE - jnp.where(v, peak, 1e30))
        part = jnp.sum(weight, axis=0, keepdims=True)
        prod = dot(vt, weight.astype(BF16), 1, 0)
        total = part if total is None else total + part
        out = prod if out is None else out + prod
    return peak, total, out


def kernel(
    table_ref,
    request_prefix_ref,
    lengths_ref,
    hidden_hbm,
    gain_hbm,
    post_gain_hbm,
    q_gain_ref,
    k_gain_ref,
    cos_ref,
    sin_ref,
    cache_ref,
    wq_hbm,
    wkv_hbm,
    wo_hbm,
    wg_hbm,
    wu_hbm,
    wd_hbm,
    out_ref,
    suffix_ref,
    hidden,
    gain,
    post_gain,
    wq,
    wkv,
    wo,
    wg,
    wu,
    wd,
    normed,
    kk,
    vt,
    q_all,
    suf,
    half_out,
    half_stat,
    res_out,
    res_stat,
    back_out,
    back_stat,
    prefix_rows,
    part,
    part_x,
    part_z,
    sent_z,
    part2,
    part2_x,
    part2_z,
    sent2_z,
    gathered,
    dma_sem,
    kv_s,
    kv_r,
    kx_s,
    kx_r,
    suf_s,
    suf_r,
    q_s,
    q_r,
    o_s,
    o_r,
    st_s,
    st_r,
    x_s,
    x_r,
    z_s,
    z_r,
    x2_s,
    x2_r,
    z2_s,
    z2_r,
    g_s,
    g_r,
):
    s = lax.axis_index("seq")
    m = lax.axis_index("mp")
    y, zh, c = lax.div(s, 4), lax.rem(lax.div(s, 2), 2), lax.rem(s, 2)
    zl, x = lax.div(m, 4), lax.rem(m, 4)

    def at_seq(i):
        return {"seq": i}

    def at_mp(i):
        return {"mp": i}

    loads = []
    for k, (src, dst) in enumerate(
        [
            (hidden_hbm, hidden),
            (gain_hbm, gain),
            (wq_hbm, wq),
            (wkv_hbm, wkv),
            (wo_hbm, wo),
            (post_gain_hbm, post_gain),
            (wg_hbm, wg),
            (wu_hbm, wu),
            (wd_hbm, wd),
        ]
    ):
        copy = pltpu.make_async_copy(src, dst, dma_sem.at[k])
        copy.start()
        loads.append(copy)

    z_peer = at_seq(y * 4 + (1 - zh) * 2 + c)
    yc_peers = []
    for dy, dc in ((0, 1), (1, 0), (1, 1), (3, 0), (3, 1), (2, 0), (2, 1)):
        yy, cc = lax.rem(y + dy, 4), lax.rem(c + dc, 2)
        yc_peers.append((cc * 4 + yy, at_seq(yy * 4 + zh * 2 + cc)))
    mine = c * 4 + y
    px = lax.rem(x, 2)
    x_partner = at_mp(zl * 4 + x + 1 - 2 * px)
    after = [at_seq(lax.rem(s + 2, SEQ)), at_seq(lax.rem(s + 1, SEQ))]
    before = [at_seq(lax.rem(s + 14, SEQ)), at_seq(lax.rem(s + 15, SEQ))]
    hops = (2, 1, 3)
    x_peers = [at_mp(zl * 4 + lax.rem(x + i, 4)) for i in hops]
    z_peers = [at_mp(lax.rem(zl + i, 4) * 4 + x) for i in hops]

    barrier = pltpu.get_barrier_semaphore()
    everyone = [z_peer] + [p for _, p in yc_peers] + after + before + x_peers + z_peers
    for dev in everyone:
        pl.semaphore_signal(barrier, inc=1, device_id=dev, device_id_type=MESH)

    lane = lax.broadcasted_iota(jnp.int32, (8, 512), 1)
    core = lax.broadcasted_iota(jnp.int32, (8, 512), 0)
    block_at = lax.shift_right_logical(lane, 7) * 4 + zh * 2 + core
    token = block_at * TOK + (lane & 127)
    own_token = s * TOK + lax.broadcasted_iota(jnp.int32, (1, TOK), 1)
    prefix = jnp.zeros((8, 512), jnp.int32)
    own_start = jnp.zeros((1, TOK), jnp.int32)
    begin = jnp.int32(0)
    for r in range(32):
        end = begin + lengths_ref[r]
        prefix = jnp.where((token >= begin) & (token < end), request_prefix_ref[r], prefix)
        own_start = jnp.where((own_token >= begin) & (own_token < end), begin, own_start)
        begin = end
    prefix_rows[...] = prefix

    slot_ids = [2 * s, 2 * s + 1, 2 * s + 4 - 8 * zh, 2 * s + 5 - 8 * zh]
    slot_prefix = [jnp.int32(0)] * 4
    for i in range(32):
        held = table_ref[i]
        slot_prefix = [
            jnp.where(held == slot, jnp.int32(i // 8), p) for slot, p in zip(slot_ids, slot_prefix)
        ]

    loads[0].wait()
    loads[1].wait()
    raw = hidden[...].astype(F32)
    normed[...] = (raw * row_scale(raw) * gain[...]).astype(BF16)

    for b in range(2):
        kk[b] = cache_ref[pl.ds(b * 256, 256), pl.ds(0, HEAD)]
        vt[b] = cache_ref[pl.ds(b * 256, 256), pl.ds(HEAD, HEAD)].T

    pl.semaphore_wait(barrier, len(everyone))

    kv_copies = [
        remote(ref.at[px], ref.at[2 + px], kv_s.at[b], kv_r.at[b], z_peer)
        for b, ref in enumerate((kk, vt))
    ]
    for copy in kv_copies:
        copy.start()

    cosine, sine = cos_ref[...], sin_ref[...]

    def head_rope(values, g):
        scaled = values * row_scale(values) * g
        return (scaled * cosine + pltpu.roll(scaled, HEAD // 2, 1) * sine).astype(BF16)

    loads[2].wait()
    q_raw = dot(normed[...], wq[...], 1, 0)
    q_all[mine] = head_rope(q_raw, q_gain_ref[...])
    q_copies = []
    for k, (_, dev) in enumerate(yc_peers):
        copy = remote(q_all.at[mine], q_all.at[mine], q_s.at[k], q_r.at[mine], dev)
        copy.start()
        q_copies.append(copy)

    loads[3].wait()
    pair = dot(normed[...], wkv[...], 1, 0).astype(BF16)
    key_rows = head_rope(pair[:, :HEAD].astype(F32), k_gain_ref[...])
    value_rows = pair[:, HEAD:]
    suf[2, 0] = key_rows
    suf[2, 1] = value_rows.T
    suffix_ref[...] = jnp.where(lax.rem(m, 2) == 0, key_rows, value_rows)

    pass_copies = []
    for b, ref in enumerate((kk, vt)):
        kv_copies[b].wait_recv()
        copy = remote(ref.at[2 + px], ref.at[2 + px], kx_s.at[b], kx_r.at[b], x_partner)
        copy.start()
        pass_copies.append(copy)

    def attend(core, first):
        return slot_part(
            [kk[first + b] for b in range(2)],
            [vt[first + b] for b in range(2)],
            q_all[pl.ds(core * 4, 4)].reshape(512, HEAD),
            [prefix_rows[pl.ds(core, 1), :] == slot_prefix[first + b] for b in range(2)],
        )

    def q_arrived(k, core):
        block = core * 4 + lax.rem(y + k, 4)
        remote(q_all.at[block], q_all.at[block], q_s.at[0], q_r.at[block], z_peer).wait_recv()

    for core in range(2):
        for k in (1, 3, 2):
            q_arrived(k, core)
        pl.when(c != core)(functools.partial(q_arrived, 0, core))
        peak, total, out = attend(core, 0)
        half_stat[core, pl.ds(0, 1), :] = peak
        half_stat[core, pl.ds(1, 1), :] = total
        half_out[core] = out

    for copy in pass_copies:
        copy.wait_recv()
    suf_copies = []
    for k in range(2):
        copy = remote(suf.at[2], suf.at[k], suf_s.at[k], suf_r.at[k], after[k])
        copy.start()
        suf_copies.append(copy)

    def send_back(k, core):
        yy = lax.rem(y + k, 4)
        block, dev = core * 4 + yy, at_seq(yy * 4 + zh * 2 + core)
        remote(res_out.at[block], back_out.at[mine], o_s.at[block], o_r.at[mine], dev).start()
        remote(res_stat.at[block], back_stat.at[mine], st_s.at[block], st_r.at[mine], dev).start()

    for core in range(2):
        peak1, total1, out1 = attend(core, 2)
        peak0 = half_stat[core, pl.ds(0, 1), :]
        total0 = half_stat[core, pl.ds(1, 1), :]
        peak = jnp.maximum(peak0, peak1)
        f0, f1 = jnp.exp2(peak0 - peak), jnp.exp2(peak1 - peak)
        total = total0 * f0 + total1 * f1
        inverse = 1.0 / jnp.maximum(total, 1.0)
        out = (half_out[core] * (f0 * inverse) + out1 * (f1 * inverse)).astype(BF16)
        for yy in range(4):
            cols = slice(yy * TOK, (yy + 1) * TOK)
            res_out[core * 4 + yy] = out[:, cols]
            res_stat[core * 4 + yy, pl.ds(0, 1), :] = peak[:, cols]
            res_stat[core * 4 + yy, pl.ds(1, 1), :] = total[:, cols]
        for k in (2, 1, 3):
            send_back(k, core)
        pl.when(c != core)(functools.partial(send_back, 0, core))

    for copy in suf_copies:
        copy.wait_recv()
    queries = q_all[mine]
    suffix_scores = []
    for k in range(3):
        at = (s - 2 + k) * TOK + lax.broadcasted_iota(jnp.int32, (TOK, TOK), 0)
        seen = (at >= own_start) & (at <= own_token)
        suffix_scores.append(
            jnp.where(seen, dot(suf[k, 0], queries, 1, 1) * SCALE, FLOOR)
        )
    suffix_peak = jnp.max(
        jnp.maximum(jnp.maximum(suffix_scores[0], suffix_scores[1]), suffix_scores[2]),
        axis=0,
        keepdims=True,
    )
    suffix_total = jnp.zeros((1, TOK), F32)
    suffix_out = jnp.zeros((HEAD, TOK), F32)
    for k in range(3):
        weight = jnp.exp2(suffix_scores[k] - suffix_peak)
        suffix_total += jnp.sum(weight, axis=0, keepdims=True)
        suffix_out += dot(suf[k, 1], weight.astype(BF16), 1, 0)

    parts = [(suffix_peak, suffix_total, suffix_out / suffix_total)]
    parts.append((res_stat[mine, pl.ds(0, 1), :], res_stat[mine, pl.ds(1, 1), :], res_out[mine]))
    for block, dev in yc_peers:
        remote(res_out.at[block], back_out.at[block], o_s.at[block], o_r.at[block], dev).wait_recv()
        remote(
            res_stat.at[block], back_stat.at[block], st_s.at[block], st_r.at[block], dev
        ).wait_recv()
        parts.append(
            (back_stat[block, pl.ds(0, 1), :], back_stat[block, pl.ds(1, 1), :], back_out[block])
        )
    best = parts[0][0]
    for peak, _, _ in parts[1:]:
        best = jnp.maximum(best, peak)
    weight_sum, accumulated = None, None
    for peak, total, out in parts:
        factor = total * jnp.exp2(peak - best)
        term = factor * out.astype(F32)
        weight_sum = factor if weight_sum is None else weight_sum + factor
        accumulated = term if accumulated is None else accumulated + term
    attended = (accumulated / weight_sum).astype(BF16)
    attended = attended.T

    def reduce_scatter(left, weight, blocks, from_x, from_z, to_z, xs, xr, zs, zr):
        sends = []
        for i in (2, 1, 3, 0):
            zz = lax.rem(zl + i, 4)
            prod = dot(left, weight[:, pl.ds(pl.multiple_of(zz * 512, 512), 512)], 1, 0)
            prod = prod.astype(BF16)
            for k in range(4):
                blocks[i, k] = prod[:, k * HEAD : (k + 1) * HEAD]
            for k, hop in enumerate(hops):
                copy = remote(
                    blocks.at[i, lax.rem(x + hop, 4)],
                    from_x.at[i, k],
                    xs.at[i, k],
                    xr.at[i, k],
                    x_peers[k],
                )
                copy.start()
                sends.append(copy)
        z_sends = []
        for n, i in enumerate((2, 1, 3, 0)):
            for k in range(3):
                sends[n * 3 + k].wait_recv()
            acc = blocks[i, x].astype(F32)
            for k in range(3):
                acc = acc + from_x[i, k].astype(F32)
            if i:
                to_z[n] = acc.astype(BF16)
                copy = remote(to_z.at[n], from_z.at[n], zs.at[n], zr.at[n], z_peers[n])
                copy.start()
                z_sends.append(copy)
        for n, copy in enumerate(z_sends):
            copy.wait_recv()
            acc = acc + from_z[n].astype(F32)
        return acc, sends + z_sends

    loads[4].wait()
    summed, sends1 = reduce_scatter(
        attended, wo, part, part_x, part_z, sent_z, x_s, x_r, z_s, z_r
    )
    columns = pl.ds(pl.multiple_of(m * HEAD, HEAD), HEAD)
    residual = (hidden[:, columns].astype(F32) + summed).astype(BF16)

    gathered[m] = residual
    g_copies = []

    def share(block, dev):
        n = len(g_copies)
        copy = remote(gathered.at[block], gathered.at[block], g_s.at[n], g_r.at[block], dev)
        copy.start()
        g_copies.append(copy)

    def arrived(block):
        remote(
            gathered.at[block], gathered.at[block], g_s.at[0], g_r.at[block], z_peers[0]
        ).wait_recv()

    for dev in z_peers:
        share(m, dev)
    for dev in x_peers:
        share(m, dev)
    for i in (1, 3, 2):
        block = lax.rem(zl + i, 4) * 4 + x
        arrived(block)
        for dev in x_peers:
            share(block, dev)
    for i in (1, 3, 2):
        for zz in range(4):
            arrived(zz * 4 + lax.rem(x + i, 4))

    square = jnp.zeros((TOK, HEAD), F32)
    for k in range(16):
        v = gathered[k].astype(F32)
        square = square + v * v
    scale = lax.rsqrt(jnp.sum(square, axis=-1, keepdims=True) * (1.0 / 2048) + EPSILON)
    loads[5].wait()
    for k in range(16):
        cols = pl.ds(k * HEAD, HEAD)
        normed[:, cols] = (gathered[k].astype(F32) * scale * post_gain[:, cols]).astype(BF16)
    loads[6].wait()
    gate = dot(normed[...], wg[...], 1, 0)
    loads[7].wait()
    up = dot(normed[...], wu[...], 1, 0)
    middle = (gate / (1.0 + jnp.exp(-gate)) * up).astype(BF16)
    loads[8].wait()
    summed, sends2 = reduce_scatter(
        middle, wd, part2, part2_x, part2_z, sent2_z, x2_s, x2_r, z2_s, z2_r
    )
    out_ref[...] = (residual.astype(F32) + summed).astype(BF16)

    for copy in kv_copies + pass_copies + suf_copies + q_copies + sends1 + sends2 + g_copies:
        copy.wait_send()
    for block, dev in yc_peers:
        remote(res_out.at[block], back_out.at[block], o_s.at[block], o_r.at[block], dev).wait_send()
        remote(
            res_stat.at[block], back_stat.at[block], st_s.at[block], st_r.at[block], dev
        ).wait_send()


def local(
    hidden_in,
    input_gain,
    w_query,
    key_value_weight,
    query_gain,
    key_gain,
    w_out,
    post_gain,
    w_gate,
    w_up,
    w_down,
    prefix_slot_cache,
    block_table,
    request_prefix,
    suffix_lengths,
):
    my_seq = lax.axis_index("seq")
    my_model = lax.axis_index("mp")
    own = my_seq * TOK + jnp.arange(TOK, dtype=jnp.int32)
    ends = jnp.cumsum(suffix_lengths)
    starts = ends - suffix_lengths
    inside = (own[:, None] >= starts[None, :]) & (own[:, None] < ends[None, :])
    start_of = jnp.sum(inside.astype(jnp.int32) * starts[None, :], axis=1)
    rotary_pos = (2048 + own - start_of).astype(F32)
    half = HEAD // 2
    inverse = jnp.exp(jnp.arange(half).astype(F32) * (-2.0 * math.log(THETA) / HEAD))
    angles = rotary_pos[:, None] * inverse[None, :]
    cosine, sine = jnp.cos(angles), jnp.sin(angles)
    cosine = jnp.concatenate([cosine, cosine], axis=1)
    sine = jnp.concatenate([-sine, sine], axis=1)
    cache = lax.dynamic_slice_in_dim(prefix_slot_cache, my_model // 2, 1, 2).reshape(512, 2 * HEAD)

    def in_hbm(value):
        return pltpu.with_memory_space_constraint(value, pltpu.HBM)

    vmem = pl.BlockSpec(memory_space=pltpu.VMEM)
    smem = pl.BlockSpec(memory_space=pltpu.SMEM)
    hbm = pl.BlockSpec(memory_space=pl.ANY)
    V = pltpu.VMEM
    D = pltpu.SemaphoreType.DMA
    block = (TOK, HEAD)
    return pl.pallas_call(
        kernel,
        out_shape=(
            jax.ShapeDtypeStruct((TOK, HEAD), BF16),
            jax.ShapeDtypeStruct((TOK, HEAD), BF16),
        ),
        in_specs=[smem] * 3 + [hbm] * 3 + [vmem] * 5 + [hbm] * 6,
        out_specs=(vmem, vmem),
        scratch_shapes=[
            V((128, 2048), BF16),
            V((1, 2048), F32),
            V((1, 2048), F32),
            V((2048, 128), BF16),
            V((2048, 256), BF16),
            V((128, 2048), BF16),
            V((2048, 384), BF16),
            V((2048, 384), BF16),
            V((384, 2048), BF16),
            V((128, 2048), BF16),
            V((4, 256, 128), BF16),
            V((4, 128, 256), BF16),
            V((8,) + block, BF16),
            V((3, 2) + block, BF16),
            V((2, 128, 512), F32),
            V((2, 8, 512), F32),
            V((8,) + block, BF16),
            V((8, 8, 128), F32),
            V((8,) + block, BF16),
            V((8, 8, 128), F32),
            V((8, 512), jnp.int32),
            V((4, 4) + block, BF16),
            V((4, 3) + block, BF16),
            V((3,) + block, BF16),
            V((3,) + block, BF16),
            V((4, 4) + block, BF16),
            V((4, 3) + block, BF16),
            V((3,) + block, BF16),
            V((3,) + block, BF16),
            V((16,) + block, BF16),
            D((9,)),
            D((2,)),
            D((2,)),
            D((2,)),
            D((2,)),
            D((2,)),
            D((2,)),
            D((7,)),
            D((8,)),
            D((8,)),
            D((8,)),
            D((8,)),
            D((8,)),
            D((4, 3)),
            D((4, 3)),
            D((3,)),
            D((3,)),
            D((4, 3)),
            D((4, 3)),
            D((3,)),
            D((3,)),
            D((15,)),
            D((16,)),
        ],
        compiler_params=pltpu.CompilerParams(
            collective_id=0, has_side_effects=True, vmem_limit_bytes=48 * 1024 * 1024
        ),
        name="layer",
    )(
        block_table,
        request_prefix,
        suffix_lengths,
        in_hbm(hidden_in),
        in_hbm(input_gain.reshape(1, -1)),
        in_hbm(post_gain.reshape(1, -1)),
        query_gain.reshape(1, -1),
        key_gain.reshape(1, -1),
        cosine,
        sine,
        cache,
        in_hbm(w_query),
        in_hbm(key_value_weight),
        in_hbm(w_out),
        in_hbm(w_gate),
        in_hbm(w_up),
        in_hbm(w_down),
    )


def solution(mesh):
    in_specs = (
        P("seq", None),
        P(),
        P(None, "mp"),
        P(None, "mp"),
        P(),
        P(),
        P("mp", None),
        P(),
        P(None, "mp"),
        P(None, "mp"),
        P("mp", None),
        P("seq", None, None, None),
        P(),
        P(),
        P(),
    )
    out_specs = (P("seq", "mp"), P("seq", "mp"))
    return jax.shard_map(local, mesh=mesh, in_specs=in_specs, out_specs=out_specs, check_vma=False)
```

```python
import functools
import math

import jax
import jax.numpy as jnp
from jax import lax
from jax.experimental import pallas as pl
from jax.experimental.pallas import tpu as pltpu
from jax.sharding import PartitionSpec as P

MESH = pl.DeviceIdType.MESH
HEAD = 128
TOK = 128
SEQ = 16
EPSILON = 1e-06
THETA = 1000000.0
FLOOR = -1e30
SCALE = math.log2(math.e) / math.sqrt(HEAD)
F32 = jnp.float32
BF16 = jnp.bfloat16


def dot(a, b, ca, cb):
    return lax.dot_general(a, b, (((ca,), (cb,)), ((), ())), preferred_element_type=F32)


def remote(src, dst, ss, rs, dev):
    return pltpu.make_async_remote_copy(
        src_ref=src, dst_ref=dst, send_sem=ss, recv_sem=rs, device_id=dev, device_id_type=MESH
    )


def row_scale(values):
    return lax.rsqrt(jnp.mean(values * values, axis=-1, keepdims=True) + EPSILON)


def slot_part(keys, values_t, queries, visible):
    scores = [dot(k, queries, 1, 1) for k in keys]
    peaks = [
        jnp.where(v, jnp.max(s, axis=0, keepdims=True) * SCALE, FLOOR)
        for s, v in zip(scores, visible)
    ]
    peak = jnp.maximum(peaks[0], peaks[1])
    total, out = None, None
    for s, v, vt in zip(scores, visible, values_t):
        weight = jnp.exp2(s * SCALE - jnp.where(v, peak, 1e30))
        part = jnp.sum(weight, axis=0, keepdims=True)
        prod = dot(vt, weight.astype(BF16), 1, 0)
        total = part if total is None else total + part
        out = prod if out is None else out + prod
    return peak, total, out


def kernel(
    table_ref,
    request_prefix_ref,
    lengths_ref,
    hidden_hbm,
    gain_hbm,
    post_gain_hbm,
    q_gain_ref,
    k_gain_ref,
    cache_ref,
    wq_hbm,
    wkv_hbm,
    wo_hbm,
    wg_hbm,
    wu_hbm,
    wd_hbm,
    out_ref,
    suffix_ref,
    hidden,
    gain,
    post_gain,
    wq,
    wkv,
    wo,
    wg,
    wu,
    wd,
    normed,
    kk,
    vt,
    q_all,
    suf,
    half_out,
    half_stat,
    res_out,
    res_stat,
    back_out,
    back_stat,
    prefix_rows,
    part,
    part_x,
    part_z,
    sent_z,
    part2,
    part2_x,
    part2_z,
    sent2_z,
    gathered,
    dma_sem,
    kv_s,
    kv_r,
    kx_s,
    kx_r,
    suf_s,
    suf_r,
    q_s,
    q_r,
    o_s,
    o_r,
    st_s,
    st_r,
    x_s,
    x_r,
    z_s,
    z_r,
    x2_s,
    x2_r,
    z2_s,
    z2_r,
    g_s,
    g_r,
    ready,
):
    s = lax.axis_index("seq")
    m = lax.axis_index("mp")
    y, zh, c = lax.div(s, 4), lax.rem(lax.div(s, 2), 2), lax.rem(s, 2)
    zl, x = lax.div(m, 4), lax.rem(m, 4)

    def at_seq(i):
        return {"seq": i}

    def at_mp(i):
        return {"mp": i}

    loads = []
    for k, (src, dst) in enumerate(
        [
            (hidden_hbm, hidden),
            (gain_hbm, gain),
            (wq_hbm, wq),
            (wkv_hbm, wkv),
            (wo_hbm, wo),
            (post_gain_hbm, post_gain),
            (wg_hbm, wg),
            (wu_hbm, wu),
            (wd_hbm, wd),
        ]
    ):
        copy = pltpu.make_async_copy(src, dst, dma_sem.at[k])
        copy.start()
        loads.append(copy)

    z_peer = at_seq(y * 4 + (1 - zh) * 2 + c)
    yc_peers = []
    for dy, dc in ((0, 1), (1, 0), (1, 1), (3, 0), (3, 1), (2, 0), (2, 1)):
        yy, cc = lax.rem(y + dy, 4), lax.rem(c + dc, 2)
        yc_peers.append((cc * 4 + yy, at_seq(yy * 4 + zh * 2 + cc)))
    mate = yc_peers[0][1]
    y_peers = [yc_peers[k] for k in (5, 1, 3)]
    mine = c * 4 + y
    px = lax.rem(x, 2)
    x_partner = at_mp(zl * 4 + x + 1 - 2 * px)
    after, before = at_seq(lax.rem(s + 2, SEQ)), at_seq(lax.rem(s + 14, SEQ))
    hops = (2, 1, 3)
    x_peers = [at_mp(zl * 4 + lax.rem(x + i, 4)) for i in hops]
    z_peers = [at_mp(lax.rem(zl + i, 4) * 4 + x) for i in hops]

    same = [z_peer, after, before] + x_peers + z_peers + [dev for _, dev in y_peers]
    barrier = pltpu.get_barrier_semaphore()
    for dev in same:
        pl.semaphore_signal(barrier, inc=1, device_id=dev, device_id_type=MESH)

    @pl.when(c == 0)
    def _():
        pl.semaphore_signal(barrier, inc=1, device_id=mate, device_id_type=MESH)

    def turn_values(slot):
        vt[slot] = cache_ref[pl.ds(pl.multiple_of(slot * 256, 256), 256), pl.ds(HEAD, HEAD)].T

    turn_values(px)
    pl.semaphore_wait(barrier, len(same) + c)

    @pl.when(c == 1)
    def _():
        pl.semaphore_signal(ready, inc=1, device_id=mate, device_id_type=MESH)

    px_rows = pl.ds(pl.multiple_of(px * 256, 256), 256)
    kv_copies = [
        remote(
            cache_ref.at[px_rows, pl.ds(0, HEAD)], kk.at[2 + px], kv_s.at[0], kv_r.at[0], z_peer
        ),
        remote(vt.at[px], vt.at[2 + px], kv_s.at[1], kv_r.at[1], z_peer),
    ]
    for copy in kv_copies:
        copy.start()
    turn_values(1 - px)

    loads[0].wait()
    loads[1].wait()
    raw = hidden[...].astype(F32)
    normed[...] = (raw * row_scale(raw) * gain[...]).astype(BF16)

    lane = lax.broadcasted_iota(jnp.int32, (8, 512), 1)
    core = lax.broadcasted_iota(jnp.int32, (8, 512), 0)
    block_at = lax.shift_right_logical(lane, 7) * 4 + zh * 2 + core
    token = block_at * TOK + (lane & 127)
    own_token = s * TOK + lax.broadcasted_iota(jnp.int32, (1, TOK), 1)
    turn_lane = lax.broadcasted_iota(jnp.int32, (64, TOK), 1)
    turn_token = s * TOK + lax.broadcasted_iota(jnp.int32, (64, TOK), 0) + (turn_lane & 64)
    turn_start = jnp.zeros((64, TOK), jnp.int32)
    prefix = jnp.zeros((8, 512), jnp.int32)
    own_start = jnp.zeros((1, TOK), jnp.int32)
    begin = jnp.int32(0)
    for r in range(32):
        end = begin + lengths_ref[r]
        prefix = jnp.where((token >= begin) & (token < end), request_prefix_ref[r], prefix)
        own_start = jnp.where((own_token >= begin) & (own_token < end), begin, own_start)
        turn_start = jnp.where((turn_token >= begin) & (turn_token < end), begin, turn_start)
        begin = end
    prefix_rows[...] = prefix

    slot_ids = [2 * s, 2 * s + 1, 2 * s + 4 - 8 * zh, 2 * s + 5 - 8 * zh]
    slot_prefix = [jnp.int32(0)] * 4
    for i in range(32):
        held = table_ref[i]
        slot_prefix = [
            jnp.where(held == slot, jnp.int32(i // 8), p) for slot, p in zip(slot_ids, slot_prefix)
        ]

    inverse = jnp.exp((turn_lane & 63).astype(F32) * (-2.0 * math.log(THETA) / HEAD))
    angles = (2048 + turn_token - turn_start).astype(F32) * inverse
    lower = turn_lane < 64

    def spread(packed):
        other = pltpu.roll(packed, HEAD // 2, 1)
        return jnp.concatenate(
            [jnp.where(lower, packed, other), jnp.where(lower, other, packed)], axis=0
        )

    cosine, sine = spread(jnp.cos(angles)), spread(jnp.sin(angles))
    half_lane = lax.broadcasted_iota(jnp.int32, (TOK, HEAD), 1)
    sine = jnp.where(half_lane < HEAD // 2, -sine, sine)

    def head_rope(values, g):
        scaled = values * row_scale(values) * g
        return (scaled * cosine + pltpu.roll(scaled, HEAD // 2, 1) * sine).astype(BF16)

    loads[2].wait()
    q_raw = dot(normed[...], wq[...], 1, 0)
    q_all[mine] = head_rope(q_raw, q_gain_ref[...])
    q_copies = []

    def send_queries(n, block, dev):
        copy = remote(q_all.at[block], q_all.at[block], q_s.at[n], q_r.at[block], dev)
        copy.start()
        q_copies.append(copy)

    for n, (_, dev) in enumerate(y_peers):
        send_queries(n, mine, dev)

    loads[3].wait()
    pair = dot(normed[...], wkv[...], 1, 0).astype(BF16)
    key_rows = head_rope(pair[:, :HEAD].astype(F32), k_gain_ref[...])
    value_rows = pair[:, HEAD:]
    suf[2, 0] = key_rows
    suf[2, 1] = value_rows.T
    suffix_ref[...] = jnp.where(lax.rem(m, 2) == 0, key_rows, value_rows)

    suf_copy = remote(suf.at[2], suf.at[0], suf_s.at[0], suf_r.at[0], after)
    suf_copy.start()

    @pl.when(c == 0)
    def _():
        pl.semaphore_wait(ready, 1)
        remote(suf.at[2], suf.at[1], suf_s.at[1], suf_r.at[1], mate).start()

    send_queries(3, mine, mate)
    for n, (block, dev) in enumerate(y_peers):
        remote(q_all.at[block], q_all.at[block], q_s.at[0], q_r.at[block], dev).wait_recv()
        send_queries(4 + n, block, mate)

    pass_copies = []
    for b, ref in enumerate((kk, vt)):
        kv_copies[b].wait_recv()
        copy = remote(ref.at[2 + px], ref.at[2 + px], kx_s.at[b], kx_r.at[b], x_partner)
        copy.start()
        pass_copies.append(copy)

    def attend(core, first, keys):
        return slot_part(
            keys,
            [vt[first + b] for b in range(2)],
            q_all[pl.ds(core * 4, 4)].reshape(512, HEAD),
            [prefix_rows[pl.ds(core, 1), :] == slot_prefix[first + b] for b in range(2)],
        )

    own_keys = [cache_ref[pl.ds(b * 256, 256), pl.ds(0, HEAD)] for b in range(2)]

    def q_arrived(core):
        for k in range(4):
            block = core * 4 + k
            remote(q_all.at[block], q_all.at[block], q_s.at[0], q_r.at[block], mate).wait_recv()

    for core in range(2):
        pl.when(c != core)(functools.partial(q_arrived, core))
        peak, total, out = attend(core, 0, own_keys)
        half_stat[core, pl.ds(0, 1), :] = peak
        half_stat[core, pl.ds(1, 1), :] = total
        half_out[core] = out

    for copy in pass_copies:
        copy.wait_recv()
    suf_copy.wait_recv()

    @pl.when(c == 1)
    def _():
        remote(suf.at[0], suf.at[1], suf_s.at[1], suf_r.at[1], mate).start()

    def send_back(k, core):
        yy = lax.rem(y + k, 4)
        block, dev = core * 4 + yy, at_seq(yy * 4 + zh * 2 + core)
        remote(res_out.at[block], back_out.at[mine], o_s.at[block], o_r.at[mine], dev).start()
        remote(res_stat.at[block], back_stat.at[mine], st_s.at[block], st_r.at[mine], dev).start()

    for core in range(2):
        peak1, total1, out1 = attend(core, 2, [kk[2], kk[3]])
        peak0 = half_stat[core, pl.ds(0, 1), :]
        total0 = half_stat[core, pl.ds(1, 1), :]
        peak = jnp.maximum(peak0, peak1)
        f0, f1 = jnp.exp2(peak0 - peak), jnp.exp2(peak1 - peak)
        total = total0 * f0 + total1 * f1
        inverse = 1.0 / jnp.maximum(total, 1.0)
        out = (half_out[core] * (f0 * inverse) + out1 * (f1 * inverse)).astype(BF16)
        for yy in range(4):
            cols = slice(yy * TOK, (yy + 1) * TOK)
            res_out[core * 4 + yy] = out[:, cols]
            res_stat[core * 4 + yy, pl.ds(0, 1), :] = peak[:, cols]
            res_stat[core * 4 + yy, pl.ds(1, 1), :] = total[:, cols]
        for k in (2, 1, 3):
            send_back(k, core)
        pl.when(c != core)(functools.partial(send_back, 0, core))

    remote(suf.at[0], suf.at[1], suf_s.at[1], suf_r.at[1], mate).wait_recv()
    queries = q_all[mine]
    suffix_scores = []
    for k in range(3):
        at = (s - 2 + k) * TOK + lax.broadcasted_iota(jnp.int32, (TOK, TOK), 0)
        seen = (at >= own_start) & (at <= own_token)
        suffix_scores.append(
            jnp.where(seen, dot(suf[k, 0], queries, 1, 1) * SCALE, FLOOR)
        )
    suffix_peak = jnp.max(
        jnp.maximum(jnp.maximum(suffix_scores[0], suffix_scores[1]), suffix_scores[2]),
        axis=0,
        keepdims=True,
    )
    suffix_total = jnp.zeros((1, TOK), F32)
    suffix_out = jnp.zeros((HEAD, TOK), F32)
    for k in range(3):
        weight = jnp.exp2(suffix_scores[k] - suffix_peak)
        suffix_total += jnp.sum(weight, axis=0, keepdims=True)
        suffix_out += dot(suf[k, 1], weight.astype(BF16), 1, 0)

    parts = [(suffix_peak, suffix_total, suffix_out / suffix_total)]
    parts.append((res_stat[mine, pl.ds(0, 1), :], res_stat[mine, pl.ds(1, 1), :], res_out[mine]))
    for block, dev in yc_peers:
        remote(res_out.at[block], back_out.at[block], o_s.at[block], o_r.at[block], dev).wait_recv()
        remote(
            res_stat.at[block], back_stat.at[block], st_s.at[block], st_r.at[block], dev
        ).wait_recv()
        parts.append(
            (back_stat[block, pl.ds(0, 1), :], back_stat[block, pl.ds(1, 1), :], back_out[block])
        )
    best = parts[0][0]
    for peak, _, _ in parts[1:]:
        best = jnp.maximum(best, peak)
    weight_sum, accumulated = None, None
    for peak, total, out in parts:
        factor = total * jnp.exp2(peak - best)
        term = factor * out.astype(F32)
        weight_sum = factor if weight_sum is None else weight_sum + factor
        accumulated = term if accumulated is None else accumulated + term
    attended = (accumulated / weight_sum).astype(BF16)
    attended = attended.T

    def reduce_scatter(left, weight, blocks, from_x, from_z, to_z, xs, xr, zs, zr):
        sends = []
        for i in (2, 1, 3, 0):
            zz = lax.rem(zl + i, 4)
            prod = dot(left, weight[:, pl.ds(pl.multiple_of(zz * 512, 512), 512)], 1, 0)
            prod = prod.astype(BF16)
            for k in range(4):
                blocks[i, k] = prod[:, k * HEAD : (k + 1) * HEAD]
            for k, hop in enumerate(hops):
                copy = remote(
                    blocks.at[i, lax.rem(x + hop, 4)],
                    from_x.at[i, k],
                    xs.at[i, k],
                    xr.at[i, k],
                    x_peers[k],
                )
                copy.start()
                sends.append(copy)
        z_sends = []
        for n, i in enumerate((2, 1, 3, 0)):
            for k in range(3):
                sends[n * 3 + k].wait_recv()
            acc = blocks[i, x].astype(F32)
            for k in range(3):
                acc = acc + from_x[i, k].astype(F32)
            if i:
                to_z[n] = acc.astype(BF16)
                copy = remote(to_z.at[n], from_z.at[n], zs.at[n], zr.at[n], z_peers[n])
                copy.start()
                z_sends.append(copy)
        for n, copy in enumerate(z_sends):
            copy.wait_recv()
            acc = acc + from_z[n].astype(F32)
        return acc, sends + z_sends

    loads[4].wait()
    summed, sends1 = reduce_scatter(
        attended, wo, part, part_x, part_z, sent_z, x_s, x_r, z_s, z_r
    )
    columns = pl.ds(pl.multiple_of(m * HEAD, HEAD), HEAD)
    residual = (hidden[:, columns].astype(F32) + summed).astype(BF16)

    gathered[m] = residual
    g_copies = []

    def share(block, dev):
        n = len(g_copies)
        copy = remote(gathered.at[block], gathered.at[block], g_s.at[n], g_r.at[block], dev)
        copy.start()
        g_copies.append(copy)

    def arrived(block):
        remote(
            gathered.at[block], gathered.at[block], g_s.at[0], g_r.at[block], z_peers[0]
        ).wait_recv()

    for dev in z_peers:
        share(m, dev)
    for dev in x_peers:
        share(m, dev)
    for i in (1, 3, 2):
        block = lax.rem(zl + i, 4) * 4 + x
        arrived(block)
        for dev in x_peers:
            share(block, dev)
    for i in (1, 3, 2):
        for zz in range(4):
            arrived(zz * 4 + lax.rem(x + i, 4))

    square = jnp.zeros((TOK, HEAD), F32)
    for k in range(16):
        v = gathered[k].astype(F32)
        square = square + v * v
    scale = lax.rsqrt(jnp.sum(square, axis=-1, keepdims=True) * (1.0 / 2048) + EPSILON)
    loads[5].wait()
    for k in range(16):
        cols = pl.ds(k * HEAD, HEAD)
        normed[:, cols] = (gathered[k].astype(F32) * scale * post_gain[:, cols]).astype(BF16)
    loads[6].wait()
    gate = dot(normed[...], wg[...], 1, 0)
    loads[7].wait()
    up = dot(normed[...], wu[...], 1, 0)
    middle = (gate / (1.0 + jnp.exp(-gate)) * up).astype(BF16)
    loads[8].wait()
    summed, sends2 = reduce_scatter(
        middle, wd, part2, part2_x, part2_z, sent2_z, x2_s, x2_r, z2_s, z2_r
    )
    out_ref[...] = (residual.astype(F32) + summed).astype(BF16)

    remote(suf.at[2], suf.at[1], suf_s.at[1], suf_r.at[1], mate).wait_send()
    for copy in kv_copies + pass_copies + [suf_copy] + q_copies + sends1 + sends2 + g_copies:
        copy.wait_send()
    for block, dev in yc_peers:
        remote(res_out.at[block], back_out.at[block], o_s.at[block], o_r.at[block], dev).wait_send()
        remote(
            res_stat.at[block], back_stat.at[block], st_s.at[block], st_r.at[block], dev
        ).wait_send()


def local(
    hidden_in,
    input_gain,
    w_query,
    key_value_weight,
    query_gain,
    key_gain,
    w_out,
    post_gain,
    w_gate,
    w_up,
    w_down,
    prefix_slot_cache,
    block_table,
    request_prefix,
    suffix_lengths,
):
    my_model = lax.axis_index("mp")
    cache = lax.dynamic_slice_in_dim(prefix_slot_cache, lax.div(my_model, 2), 1, 2).reshape(512, 2 * HEAD)

    def in_hbm(value):
        return pltpu.with_memory_space_constraint(value, pltpu.HBM)

    vmem = pl.BlockSpec(memory_space=pltpu.VMEM)
    smem = pl.BlockSpec(memory_space=pltpu.SMEM)
    hbm = pl.BlockSpec(memory_space=pl.ANY)
    V = pltpu.VMEM
    D = pltpu.SemaphoreType.DMA
    block = (TOK, HEAD)
    return pl.pallas_call(
        kernel,
        out_shape=(
            jax.ShapeDtypeStruct((TOK, HEAD), BF16),
            jax.ShapeDtypeStruct((TOK, HEAD), BF16),
        ),
        in_specs=[smem] * 3 + [hbm] * 3 + [vmem] * 3 + [hbm] * 6,
        out_specs=(vmem, vmem),
        scratch_shapes=[
            V((128, 2048), BF16),
            V((1, 2048), F32),
            V((1, 2048), F32),
            V((2048, 128), BF16),
            V((2048, 256), BF16),
            V((128, 2048), BF16),
            V((2048, 384), BF16),
            V((2048, 384), BF16),
            V((384, 2048), BF16),
            V((128, 2048), BF16),
            V((4, 256, 128), BF16),
            V((4, 128, 256), BF16),
            V((8,) + block, BF16),
            V((3, 2) + block, BF16),
            V((2, 128, 512), F32),
            V((2, 8, 512), F32),
            V((8,) + block, BF16),
            V((8, 8, 128), F32),
            V((8,) + block, BF16),
            V((8, 8, 128), F32),
            V((8, 512), jnp.int32),
            V((4, 4) + block, BF16),
            V((4, 3) + block, BF16),
            V((3,) + block, BF16),
            V((3,) + block, BF16),
            V((4, 4) + block, BF16),
            V((4, 3) + block, BF16),
            V((3,) + block, BF16),
            V((3,) + block, BF16),
            V((16,) + block, BF16),
            D((9,)),
            D((2,)),
            D((2,)),
            D((2,)),
            D((2,)),
            D((2,)),
            D((2,)),
            D((7,)),
            D((8,)),
            D((8,)),
            D((8,)),
            D((8,)),
            D((8,)),
            D((4, 3)),
            D((4, 3)),
            D((3,)),
            D((3,)),
            D((4, 3)),
            D((4, 3)),
            D((3,)),
            D((3,)),
            D((15,)),
            D((16,)),
            pltpu.SemaphoreType.REGULAR,
        ],
        compiler_params=pltpu.CompilerParams(
            collective_id=0, has_side_effects=True, vmem_limit_bytes=48 * 1024 * 1024
        ),
        name="layer",
    )(
        block_table,
        request_prefix,
        suffix_lengths,
        in_hbm(hidden_in),
        in_hbm(input_gain.reshape(1, -1)),
        in_hbm(post_gain.reshape(1, -1)),
        query_gain.reshape(1, -1),
        key_gain.reshape(1, -1),
        cache,
        in_hbm(w_query),
        in_hbm(key_value_weight),
        in_hbm(w_out),
        in_hbm(w_gate),
        in_hbm(w_up),
        in_hbm(w_down),
    )


def solution(mesh):
    in_specs = (
        P("seq", None),
        P(),
        P(None, "mp"),
        P(None, "mp"),
        P(),
        P(),
        P("mp", None),
        P(),
        P(None, "mp"),
        P(None, "mp"),
        P("mp", None),
        P("seq", None, None, None),
        P(),
        P(),
        P(),
    )
    out_specs = (P("seq", "mp"), P("seq", "mp"))
    return jax.shard_map(local, mesh=mesh, in_specs=in_specs, out_specs=out_specs, check_vma=False)
```

```python
import functools
import math

import jax
import jax.numpy as jnp
from jax import lax
from jax.experimental import pallas as pl
from jax.experimental.pallas import tpu as pltpu
from jax.sharding import PartitionSpec as P

MESH = pl.DeviceIdType.MESH
HEAD = 128
TOK = 128
SEQ = 16
EPSILON = 1e-06
THETA = 1000000.0
FLOOR = -1e30
SCALE = math.log2(math.e) / math.sqrt(HEAD)
F32 = jnp.float32
BF16 = jnp.bfloat16


def dot(a, b, ca, cb):
    return lax.dot_general(a, b, (((ca,), (cb,)), ((), ())), preferred_element_type=F32)


def remote(src, dst, ss, rs, dev):
    return pltpu.make_async_remote_copy(
        src_ref=src, dst_ref=dst, send_sem=ss, recv_sem=rs, device_id=dev, device_id_type=MESH
    )


def row_scale(values):
    return lax.rsqrt(jnp.mean(values * values, axis=-1, keepdims=True) + EPSILON)


def slot_part(keys, values_t, queries, visible):
    scores = [dot(k, queries, 1, 1) for k in keys]
    peaks = [
        jnp.where(v, jnp.max(s, axis=0, keepdims=True) * SCALE, FLOOR)
        for s, v in zip(scores, visible)
    ]
    peak = jnp.maximum(peaks[0], peaks[1])
    total, out = None, None
    for s, v, vt in zip(scores, visible, values_t):
        weight = jnp.exp2(s * SCALE - jnp.where(v, peak, 1e30))
        part = jnp.sum(weight, axis=0, keepdims=True)
        prod = dot(vt, weight.astype(BF16), 1, 0)
        total = part if total is None else total + part
        out = prod if out is None else out + prod
    return peak, total, out


def kernel(
    table_ref,
    request_prefix_ref,
    lengths_ref,
    hidden_hbm,
    gain_hbm,
    post_gain_hbm,
    q_gain_ref,
    k_gain_ref,
    cache_ref,
    wq_hbm,
    wkv_hbm,
    wo_hbm,
    wg_hbm,
    wu_hbm,
    wd_hbm,
    out_ref,
    suffix_ref,
    hidden,
    gain,
    post_gain,
    wq,
    wkv,
    wo,
    wg,
    wu,
    wd,
    normed,
    kk,
    vt,
    q_all,
    suf,
    half_out,
    half_stat,
    res_out,
    res_stat,
    back_out,
    back_stat,
    prefix_rows,
    part,
    part_x,
    part_z,
    sent_z,
    part2,
    part2_x,
    part2_z,
    sent2_z,
    gathered,
    dma_sem,
    kv_s,
    kv_r,
    kx_s,
    kx_r,
    suf_s,
    suf_r,
    q_s,
    q_r,
    o_s,
    o_r,
    st_s,
    st_r,
    x_s,
    x_r,
    z_s,
    z_r,
    x2_s,
    x2_r,
    z2_s,
    z2_r,
    g_s,
    g_r,
    ready,
):
    s = lax.axis_index("seq")
    m = lax.axis_index("mp")
    y, zh, c = lax.div(s, 4), lax.rem(lax.div(s, 2), 2), lax.rem(s, 2)
    zl, x = lax.div(m, 4), lax.rem(m, 4)

    def at_seq(i):
        return {"seq": i}

    def at_mp(i):
        return {"mp": i}

    loads = []
    for k, (src, dst) in enumerate(
        [
            (hidden_hbm, hidden),
            (gain_hbm, gain),
            (wq_hbm, wq),
            (wkv_hbm, wkv),
            (wo_hbm, wo),
            (post_gain_hbm, post_gain),
            (wg_hbm, wg),
            (wu_hbm, wu),
            (wd_hbm, wd),
        ]
    ):
        copy = pltpu.make_async_copy(src, dst, dma_sem.at[k])
        copy.start()
        loads.append(copy)

    z_peer = at_seq(y * 4 + (1 - zh) * 2 + c)
    yc_peers = []
    for dy, dc in ((0, 1), (1, 0), (1, 1), (3, 0), (3, 1), (2, 0), (2, 1)):
        yy, cc = lax.rem(y + dy, 4), lax.rem(c + dc, 2)
        yc_peers.append((cc * 4 + yy, at_seq(yy * 4 + zh * 2 + cc)))
    mate = yc_peers[0][1]
    y_peers = [yc_peers[k] for k in (5, 1, 3)]
    mine = c * 4 + y
    px = lax.rem(x, 2)
    x_partner = at_mp(zl * 4 + x + 1 - 2 * px)
    after, before = at_seq(lax.rem(s + 2, SEQ)), at_seq(lax.rem(s + 14, SEQ))
    hops = (2, 1, 3)
    x_peers = [at_mp(zl * 4 + lax.rem(x + i, 4)) for i in hops]
    z_peers = [at_mp(lax.rem(zl + i, 4) * 4 + x) for i in hops]

    same = [z_peer, after, before] + x_peers + z_peers + [dev for _, dev in y_peers]
    barrier = pltpu.get_barrier_semaphore()
    for dev in same:
        pl.semaphore_signal(barrier, inc=1, device_id=dev, device_id_type=MESH)

    @pl.when(c == 0)
    def _():
        pl.semaphore_signal(barrier, inc=1, device_id=mate, device_id_type=MESH)

    def turn_values(slot):
        vt[slot] = cache_ref[pl.ds(pl.multiple_of(slot * 256, 256), 256), pl.ds(HEAD, HEAD)].T

    turn_values(px)
    pl.semaphore_wait(barrier, len(same) + c)

    @pl.when(c == 1)
    def _():
        pl.semaphore_signal(ready, inc=1, device_id=mate, device_id_type=MESH)

    px_rows = pl.ds(pl.multiple_of(px * 256, 256), 256)
    kv_copies = [
        remote(
            cache_ref.at[px_rows, pl.ds(0, HEAD)], kk.at[2 + px], kv_s.at[0], kv_r.at[0], z_peer
        ),
        remote(vt.at[px], vt.at[2 + px], kv_s.at[1], kv_r.at[1], z_peer),
    ]
    for copy in kv_copies:
        copy.start()
    turn_values(1 - px)

    loads[0].wait()
    loads[1].wait()
    raw = hidden[...].astype(F32)
    normed[...] = (raw * row_scale(raw) * gain[...]).astype(BF16)

    lane = lax.broadcasted_iota(jnp.int32, (8, 512), 1)
    core = lax.broadcasted_iota(jnp.int32, (8, 512), 0)
    block_at = lax.shift_right_logical(lane, 7) * 4 + zh * 2 + core
    token = block_at * TOK + (lane & 127)
    own_token = s * TOK + lax.broadcasted_iota(jnp.int32, (1, TOK), 1)
    turn_lane = lax.broadcasted_iota(jnp.int32, (64, TOK), 1)
    turn_token = s * TOK + lax.broadcasted_iota(jnp.int32, (64, TOK), 0) + (turn_lane & 64)
    turn_start = jnp.zeros((64, TOK), jnp.int32)
    prefix = jnp.zeros((8, 512), jnp.int32)
    own_start = jnp.zeros((1, TOK), jnp.int32)
    begin = jnp.int32(0)
    for r in range(32):
        end = begin + lengths_ref[r]
        prefix = jnp.where((token >= begin) & (token < end), request_prefix_ref[r], prefix)
        own_start = jnp.where((own_token >= begin) & (own_token < end), begin, own_start)
        turn_start = jnp.where((turn_token >= begin) & (turn_token < end), begin, turn_start)
        begin = end
    prefix_rows[...] = prefix

    slot_ids = [2 * s, 2 * s + 1, 2 * s + 4 - 8 * zh, 2 * s + 5 - 8 * zh]
    slot_prefix = [jnp.int32(0)] * 4
    for i in range(32):
        held = table_ref[i]
        slot_prefix = [
            jnp.where(held == slot, jnp.int32(i // 8), p) for slot, p in zip(slot_ids, slot_prefix)
        ]

    inverse = jnp.exp((turn_lane & 63).astype(F32) * (-2.0 * math.log(THETA) / HEAD))
    angles = (2048 + turn_token - turn_start).astype(F32) * inverse
    lower = turn_lane < 64

    def spread(packed):
        other = pltpu.roll(packed, HEAD // 2, 1)
        return jnp.concatenate(
            [jnp.where(lower, packed, other), jnp.where(lower, other, packed)], axis=0
        )

    cosine, sine = spread(jnp.cos(angles)), spread(jnp.sin(angles))
    half_lane = lax.broadcasted_iota(jnp.int32, (TOK, HEAD), 1)
    sine = jnp.where(half_lane < HEAD // 2, -sine, sine)

    def head_rope(values, g):
        scaled = values * row_scale(values) * g
        return (scaled * cosine + pltpu.roll(scaled, HEAD // 2, 1) * sine).astype(BF16)

    loads[2].wait()
    q_raw = dot(normed[...], wq[...], 1, 0)
    q_all[mine] = head_rope(q_raw, q_gain_ref[...])
    q_copies = []

    def send_queries(n, block, dev):
        copy = remote(q_all.at[block], q_all.at[block], q_s.at[n], q_r.at[block], dev)
        copy.start()
        q_copies.append(copy)

    for n, (_, dev) in enumerate(y_peers):
        send_queries(n, mine, dev)

    loads[3].wait()
    pair = dot(normed[...], wkv[...], 1, 0).astype(BF16)
    key_rows = head_rope(pair[:, :HEAD].astype(F32), k_gain_ref[...])
    value_rows = pair[:, HEAD:]
    suf[2, 0] = key_rows
    suf[2, 1] = value_rows.T
    suffix_ref[...] = jnp.where(lax.rem(m, 2) == 0, key_rows, value_rows)

    suf_copy = remote(suf.at[2], suf.at[0], suf_s.at[0], suf_r.at[0], after)
    suf_copy.start()

    @pl.when(c == 0)
    def _():
        pl.semaphore_wait(ready, 1)
        remote(suf.at[2], suf.at[1], suf_s.at[1], suf_r.at[1], mate).start()

    send_queries(3, mine, mate)
    for n, (block, dev) in enumerate(y_peers):
        remote(q_all.at[block], q_all.at[block], q_s.at[0], q_r.at[block], dev).wait_recv()
        send_queries(4 + n, block, mate)

    pass_copies = []
    for b, ref in enumerate((kk, vt)):
        kv_copies[b].wait_recv()
        copy = remote(ref.at[2 + px], ref.at[2 + px], kx_s.at[b], kx_r.at[b], x_partner)
        copy.start()
        pass_copies.append(copy)

    def attend(core, first, keys):
        return slot_part(
            keys,
            [vt[first + b] for b in range(2)],
            q_all[pl.ds(core * 4, 4)].reshape(512, HEAD),
            [prefix_rows[pl.ds(core, 1), :] == slot_prefix[first + b] for b in range(2)],
        )

    own_keys = [cache_ref[pl.ds(b * 256, 256), pl.ds(0, HEAD)] for b in range(2)]

    def q_arrived(core):
        for k in range(4):
            block = core * 4 + k
            remote(q_all.at[block], q_all.at[block], q_s.at[0], q_r.at[block], mate).wait_recv()

    for core in range(2):
        pl.when(c != core)(functools.partial(q_arrived, core))
        peak, total, out = attend(core, 0, own_keys)
        half_stat[core, pl.ds(0, 1), :] = peak
        half_stat[core, pl.ds(1, 1), :] = total
        half_out[core] = out

    for copy in pass_copies:
        copy.wait_recv()
    suf_copy.wait_recv()

    @pl.when(c == 1)
    def _():
        remote(suf.at[0], suf.at[1], suf_s.at[1], suf_r.at[1], mate).start()

    def send_back(k, core):
        yy = lax.rem(y + k, 4)
        block, dev = core * 4 + yy, at_seq(yy * 4 + zh * 2 + core)
        remote(res_out.at[block], back_out.at[mine], o_s.at[block], o_r.at[mine], dev).start()
        remote(res_stat.at[block], back_stat.at[mine], st_s.at[block], st_r.at[mine], dev).start()

    for core in range(2):
        peak1, total1, out1 = attend(core, 2, [kk[2], kk[3]])
        peak0 = half_stat[core, pl.ds(0, 1), :]
        total0 = half_stat[core, pl.ds(1, 1), :]
        peak = jnp.maximum(peak0, peak1)
        f0, f1 = jnp.exp2(peak0 - peak), jnp.exp2(peak1 - peak)
        total = total0 * f0 + total1 * f1
        inverse = 1.0 / jnp.maximum(total, 1.0)
        out = (half_out[core] * (f0 * inverse) + out1 * (f1 * inverse)).astype(BF16)
        for yy in range(4):
            cols = slice(yy * TOK, (yy + 1) * TOK)
            res_out[core * 4 + yy] = out[:, cols]
            res_stat[core * 4 + yy, pl.ds(0, 1), :] = peak[:, cols]
            res_stat[core * 4 + yy, pl.ds(1, 1), :] = total[:, cols]
        for k in (2, 1, 3):
            send_back(k, core)
        pl.when(c != core)(functools.partial(send_back, 0, core))

    remote(suf.at[0], suf.at[1], suf_s.at[1], suf_r.at[1], mate).wait_recv()
    queries = q_all[mine]
    suffix_scores = []
    for k in range(3):
        at = (s - 2 + k) * TOK + lax.broadcasted_iota(jnp.int32, (TOK, TOK), 0)
        seen = (at >= own_start) & (at <= own_token)
        suffix_scores.append(
            jnp.where(seen, dot(suf[k, 0], queries, 1, 1) * SCALE, FLOOR)
        )
    suffix_peak = jnp.max(
        jnp.maximum(jnp.maximum(suffix_scores[0], suffix_scores[1]), suffix_scores[2]),
        axis=0,
        keepdims=True,
    )
    suffix_total = jnp.zeros((1, TOK), F32)
    suffix_out = jnp.zeros((HEAD, TOK), F32)
    for k in range(3):
        weight = jnp.exp2(suffix_scores[k] - suffix_peak)
        suffix_total += jnp.sum(weight, axis=0, keepdims=True)
        suffix_out += dot(suf[k, 1], weight.astype(BF16), 1, 0)

    parts = [(suffix_peak, suffix_total, suffix_out / suffix_total)]
    parts.append((res_stat[mine, pl.ds(0, 1), :], res_stat[mine, pl.ds(1, 1), :], res_out[mine]))
    for block, dev in yc_peers:
        remote(res_out.at[block], back_out.at[block], o_s.at[block], o_r.at[block], dev).wait_recv()
        remote(
            res_stat.at[block], back_stat.at[block], st_s.at[block], st_r.at[block], dev
        ).wait_recv()
        parts.append(
            (back_stat[block, pl.ds(0, 1), :], back_stat[block, pl.ds(1, 1), :], back_out[block])
        )
    best = parts[0][0]
    for peak, _, _ in parts[1:]:
        best = jnp.maximum(best, peak)
    weight_sum, accumulated = None, None
    for peak, total, out in parts:
        factor = total * jnp.exp2(peak - best)
        term = factor * out.astype(F32)
        weight_sum = factor if weight_sum is None else weight_sum + factor
        accumulated = term if accumulated is None else accumulated + term
    attended = (accumulated / weight_sum).astype(BF16)
    attended = attended.T

    def reduce_scatter(left, weight, blocks, from_x, from_z, to_z, xs, xr, zs, zr):
        sends = []
        for i in (2, 1, 3, 0):
            zz = lax.rem(zl + i, 4)
            prod = dot(left, weight[:, pl.ds(pl.multiple_of(zz * 512, 512), 512)], 1, 0)
            prod = prod.astype(BF16)
            for k in range(4):
                blocks[i, k] = prod[:, k * HEAD : (k + 1) * HEAD]
            for k, hop in enumerate(hops):
                copy = remote(
                    blocks.at[i, lax.rem(x + hop, 4)],
                    from_x.at[i, k],
                    xs.at[i, k],
                    xr.at[i, k],
                    x_peers[k],
                )
                copy.start()
                sends.append(copy)
        z_sends = []
        for n, i in enumerate((2, 1, 3, 0)):
            for k in range(3):
                sends[n * 3 + k].wait_recv()
            acc = blocks[i, x].astype(F32)
            for k in range(3):
                acc = acc + from_x[i, k].astype(F32)
            if i:
                to_z[n] = acc.astype(BF16)
                copy = remote(to_z.at[n], from_z.at[n], zs.at[n], zr.at[n], z_peers[n])
                copy.start()
                z_sends.append(copy)
        for n, copy in enumerate(z_sends):
            copy.wait_recv()
            acc = acc + from_z[n].astype(F32)
        return acc, sends + z_sends

    loads[4].wait()
    summed, sends1 = reduce_scatter(
        attended, wo, part, part_x, part_z, sent_z, x_s, x_r, z_s, z_r
    )
    columns = pl.ds(pl.multiple_of(m * HEAD, HEAD), HEAD)
    residual = (hidden[:, columns].astype(F32) + summed).astype(BF16)

    gathered[m] = residual
    g_copies = []

    def share(block, dev):
        n = len(g_copies)
        copy = remote(gathered.at[block], gathered.at[block], g_s.at[n], g_r.at[block], dev)
        copy.start()
        g_copies.append(copy)

    def arrived(block):
        remote(
            gathered.at[block], gathered.at[block], g_s.at[0], g_r.at[block], z_peers[0]
        ).wait_recv()

    z_rows = [zl, zl + 1 - 2 * lax.rem(zl, 2), lax.rem(zl + 2, 4), 3 - zl]
    for i in (3, 2, 1):
        share(m, at_mp(z_rows[i] * 4 + x))
    for dev in x_peers:
        share(m, dev)
    for i in (1, 2, 3):
        arrived(z_rows[i] * 4 + x)
        for dev in x_peers:
            share(z_rows[i] * 4 + x, dev)
    for k in (5, 6, 7):
        loads[k].wait()
    square = jnp.zeros((TOK, HEAD), F32)
    gate, up = None, None
    for i in range(4):
        for hop in (1, 3, 2):
            arrived(z_rows[i] * 4 + lax.rem(x + hop, 4))
        base = z_rows[i] * 4
        scaled = []
        for k in range(4):
            v = gathered[base + k].astype(F32)
            square = square + v * v
            cols = pl.ds(pl.multiple_of((base + k) * HEAD, HEAD), HEAD)
            scaled.append((v * post_gain[:, cols]).astype(BF16))
        scaled = jnp.concatenate(scaled, axis=1)
        rows = pl.ds(pl.multiple_of(base * HEAD, 4 * HEAD), 4 * HEAD)
        gate_part, up_part = dot(scaled, wg[rows, :], 1, 0), dot(scaled, wu[rows, :], 1, 0)
        gate = gate_part if gate is None else gate + gate_part
        up = up_part if up is None else up + up_part
    scale = lax.rsqrt(jnp.sum(square, axis=-1, keepdims=True) * (1.0 / 2048) + EPSILON)
    gate, up = gate * scale, up * scale
    middle = (gate / (1.0 + jnp.exp(-gate)) * up).astype(BF16)
    loads[8].wait()
    summed, sends2 = reduce_scatter(
        middle, wd, part2, part2_x, part2_z, sent2_z, x2_s, x2_r, z2_s, z2_r
    )
    out_ref[...] = (residual.astype(F32) + summed).astype(BF16)

    remote(suf.at[2], suf.at[1], suf_s.at[1], suf_r.at[1], mate).wait_send()
    for copy in kv_copies + pass_copies + [suf_copy] + q_copies + sends1 + sends2 + g_copies:
        copy.wait_send()
    for block, dev in yc_peers:
        remote(res_out.at[block], back_out.at[block], o_s.at[block], o_r.at[block], dev).wait_send()
        remote(
            res_stat.at[block], back_stat.at[block], st_s.at[block], st_r.at[block], dev
        ).wait_send()


def local(
    hidden_in,
    input_gain,
    w_query,
    key_value_weight,
    query_gain,
    key_gain,
    w_out,
    post_gain,
    w_gate,
    w_up,
    w_down,
    prefix_slot_cache,
    block_table,
    request_prefix,
    suffix_lengths,
):
    my_model = lax.axis_index("mp")
    cache = lax.dynamic_slice_in_dim(prefix_slot_cache, lax.div(my_model, 2), 1, 2).reshape(512, 2 * HEAD)

    def in_hbm(value):
        return pltpu.with_memory_space_constraint(value, pltpu.HBM)

    vmem = pl.BlockSpec(memory_space=pltpu.VMEM)
    smem = pl.BlockSpec(memory_space=pltpu.SMEM)
    hbm = pl.BlockSpec(memory_space=pl.ANY)
    V = pltpu.VMEM
    D = pltpu.SemaphoreType.DMA
    block = (TOK, HEAD)
    return pl.pallas_call(
        kernel,
        out_shape=(
            jax.ShapeDtypeStruct((TOK, HEAD), BF16),
            jax.ShapeDtypeStruct((TOK, HEAD), BF16),
        ),
        in_specs=[smem] * 3 + [hbm] * 3 + [vmem] * 3 + [hbm] * 6,
        out_specs=(vmem, vmem),
        scratch_shapes=[
            V((128, 2048), BF16),
            V((1, 2048), F32),
            V((1, 2048), F32),
            V((2048, 128), BF16),
            V((2048, 256), BF16),
            V((128, 2048), BF16),
            V((2048, 384), BF16),
            V((2048, 384), BF16),
            V((384, 2048), BF16),
            V((128, 2048), BF16),
            V((4, 256, 128), BF16),
            V((4, 128, 256), BF16),
            V((8,) + block, BF16),
            V((3, 2) + block, BF16),
            V((2, 128, 512), F32),
            V((2, 8, 512), F32),
            V((8,) + block, BF16),
            V((8, 8, 128), F32),
            V((8,) + block, BF16),
            V((8, 8, 128), F32),
            V((8, 512), jnp.int32),
            V((4, 4) + block, BF16),
            V((4, 3) + block, BF16),
            V((3,) + block, BF16),
            V((3,) + block, BF16),
            V((4, 4) + block, BF16),
            V((4, 3) + block, BF16),
            V((3,) + block, BF16),
            V((3,) + block, BF16),
            V((16,) + block, BF16),
            D((9,)),
            D((2,)),
            D((2,)),
            D((2,)),
            D((2,)),
            D((2,)),
            D((2,)),
            D((7,)),
            D((8,)),
            D((8,)),
            D((8,)),
            D((8,)),
            D((8,)),
            D((4, 3)),
            D((4, 3)),
            D((3,)),
            D((3,)),
            D((4, 3)),
            D((4, 3)),
            D((3,)),
            D((3,)),
            D((15,)),
            D((16,)),
            pltpu.SemaphoreType.REGULAR,
        ],
        compiler_params=pltpu.CompilerParams(
            collective_id=0, has_side_effects=True, vmem_limit_bytes=48 * 1024 * 1024
        ),
        name="layer",
    )(
        block_table,
        request_prefix,
        suffix_lengths,
        in_hbm(hidden_in),
        in_hbm(input_gain.reshape(1, -1)),
        in_hbm(post_gain.reshape(1, -1)),
        query_gain.reshape(1, -1),
        key_gain.reshape(1, -1),
        cache,
        in_hbm(w_query),
        in_hbm(key_value_weight),
        in_hbm(w_out),
        in_hbm(w_gate),
        in_hbm(w_up),
        in_hbm(w_down),
    )


def solution(mesh):
    in_specs = (
        P("seq", None),
        P(),
        P(None, "mp"),
        P(None, "mp"),
        P(),
        P(),
        P("mp", None),
        P(),
        P(None, "mp"),
        P(None, "mp"),
        P("mp", None),
        P("seq", None, None, None),
        P(),
        P(),
        P(),
    )
    out_specs = (P("seq", "mp"), P("seq", "mp"))
    return jax.shard_map(local, mesh=mesh, in_specs=in_specs, out_specs=out_specs, check_vma=False)
```

```python
import functools
import math

import jax
import jax.numpy as jnp
from jax import lax
from jax.experimental import pallas as pl
from jax.experimental.pallas import tpu as pltpu
from jax.sharding import PartitionSpec as P

MESH = pl.DeviceIdType.MESH
HEAD = 128
TOK = 128
SEQ = 16
EPSILON = 1e-06
THETA = 1000000.0
FLOOR = -1e30
SCALE = math.log2(math.e) / math.sqrt(HEAD)
F32 = jnp.float32
BF16 = jnp.bfloat16


def dot(a, b, ca, cb):
    return lax.dot_general(a, b, (((ca,), (cb,)), ((), ())), preferred_element_type=F32)


def remote(src, dst, ss, rs, dev):
    return pltpu.make_async_remote_copy(
        src_ref=src, dst_ref=dst, send_sem=ss, recv_sem=rs, device_id=dev, device_id_type=MESH
    )


def row_scale(values):
    return lax.rsqrt(jnp.mean(values * values, axis=-1, keepdims=True) + EPSILON)


def slot_part(keys, values_t, queries, visible):
    scores = [dot(k, queries, 1, 1) for k in keys]
    peaks = [
        jnp.where(v, jnp.max(s, axis=0, keepdims=True) * SCALE, FLOOR)
        for s, v in zip(scores, visible)
    ]
    peak = jnp.maximum(peaks[0], peaks[1])
    total, out = None, None
    for s, v, vt in zip(scores, visible, values_t):
        weight = jnp.exp2(s * SCALE - jnp.where(v, peak, 1e30))
        part = jnp.sum(weight, axis=0, keepdims=True)
        prod = dot(vt, weight.astype(BF16), 1, 0)
        total = part if total is None else total + part
        out = prod if out is None else out + prod
    return peak, total, out


def kernel(
    table_ref,
    request_prefix_ref,
    lengths_ref,
    hidden_hbm,
    gain_hbm,
    post_gain_hbm,
    q_gain_ref,
    k_gain_ref,
    cache_ref,
    wq_hbm,
    wkv_hbm,
    wo_hbm,
    wg_hbm,
    wu_hbm,
    wd_hbm,
    out_ref,
    hidden,
    gain,
    post_gain,
    wq,
    wkv,
    wo,
    wg,
    wu,
    wd,
    normed,
    kk,
    vt,
    q_all,
    suf,
    half_out,
    half_stat,
    res_out,
    res_stat,
    back_out,
    back_stat,
    prefix_rows,
    part,
    part_x,
    part_z,
    sent_z,
    part2,
    part2_x,
    part2_z,
    sent2_z,
    gathered,
    dma_sem,
    kv_s,
    kv_r,
    kx_s,
    kx_r,
    suf_s,
    suf_r,
    q_s,
    q_r,
    o_s,
    o_r,
    st_s,
    st_r,
    x_s,
    x_r,
    z_s,
    z_r,
    x2_s,
    x2_r,
    z2_s,
    z2_r,
    g_s,
    g_r,
    ready,
):
    s = lax.axis_index("seq")
    m = lax.axis_index("mp")
    y, zh, c = lax.div(s, 4), lax.rem(lax.div(s, 2), 2), lax.rem(s, 2)
    zl, x = lax.div(m, 4), lax.rem(m, 4)

    def at_seq(i):
        return {"seq": i}

    def at_mp(i):
        return {"mp": i}

    loads = []
    for k, (src, dst) in enumerate(
        [
            (hidden_hbm, hidden),
            (gain_hbm, gain),
            (wq_hbm, wq),
            (wkv_hbm, wkv),
            (wo_hbm, wo),
            (post_gain_hbm, post_gain),
            (wg_hbm, wg),
            (wu_hbm, wu),
            (wd_hbm, wd),
        ]
    ):
        copy = pltpu.make_async_copy(src, dst, dma_sem.at[k])
        copy.start()
        loads.append(copy)

    z_peer = at_seq(y * 4 + (1 - zh) * 2 + c)
    yc_peers = []
    for dy, dc in ((0, 1), (1, 0), (1, 1), (3, 0), (3, 1), (2, 0), (2, 1)):
        yy, cc = lax.rem(y + dy, 4), lax.rem(c + dc, 2)
        yc_peers.append((cc * 4 + yy, at_seq(yy * 4 + zh * 2 + cc)))
    mate = yc_peers[0][1]
    y_peers = [yc_peers[k] for k in (5, 1, 3)]
    mine = c * 4 + y
    px = lax.rem(x, 2)
    x_partner = at_mp(zl * 4 + x + 1 - 2 * px)
    after, before = at_seq(lax.rem(s + 2, SEQ)), at_seq(lax.rem(s + 14, SEQ))
    hops = (2, 1, 3)
    x_peers = [at_mp(zl * 4 + lax.rem(x + i, 4)) for i in hops]
    z_peers = [at_mp(lax.rem(zl + i, 4) * 4 + x) for i in hops]

    same = [z_peer, after, before] + x_peers + z_peers + [dev for _, dev in y_peers]
    barrier = pltpu.get_barrier_semaphore()
    for dev in same:
        pl.semaphore_signal(barrier, inc=1, device_id=dev, device_id_type=MESH)

    @pl.when(c == 0)
    def _():
        pl.semaphore_signal(barrier, inc=1, device_id=mate, device_id_type=MESH)

    def turn_values(slot):
        vt[slot] = cache_ref[pl.ds(pl.multiple_of(slot * 256, 256), 256), pl.ds(HEAD, HEAD)].T

    turn_values(px)
    pl.semaphore_wait(barrier, len(same) + c)

    @pl.when(c == 1)
    def _():
        pl.semaphore_signal(ready, inc=1, device_id=mate, device_id_type=MESH)

    px_rows = pl.ds(pl.multiple_of(px * 256, 256), 256)
    kv_copies = [
        remote(
            cache_ref.at[px_rows, pl.ds(0, HEAD)], kk.at[2 + px], kv_s.at[0], kv_r.at[0], z_peer
        ),
        remote(vt.at[px], vt.at[2 + px], kv_s.at[1], kv_r.at[1], z_peer),
    ]
    for copy in kv_copies:
        copy.start()
    turn_values(1 - px)

    loads[0].wait()
    loads[1].wait()
    raw = hidden[...].astype(F32)
    normed[...] = (raw * row_scale(raw) * gain[...]).astype(BF16)

    lane = lax.broadcasted_iota(jnp.int32, (8, 512), 1)
    core = lax.broadcasted_iota(jnp.int32, (8, 512), 0)
    block_at = lax.shift_right_logical(lane, 7) * 4 + zh * 2 + core
    token = block_at * TOK + (lane & 127)
    own_token = s * TOK + lax.broadcasted_iota(jnp.int32, (1, TOK), 1)
    turn_lane = lax.broadcasted_iota(jnp.int32, (64, TOK), 1)
    turn_token = s * TOK + lax.broadcasted_iota(jnp.int32, (64, TOK), 0) + (turn_lane & 64)
    turn_start = jnp.zeros((64, TOK), jnp.int32)
    prefix = jnp.zeros((8, 512), jnp.int32)
    own_start = jnp.zeros((1, TOK), jnp.int32)
    begin = jnp.int32(0)
    for r in range(32):
        end = begin + lengths_ref[r]
        prefix = jnp.where((token >= begin) & (token < end), request_prefix_ref[r], prefix)
        own_start = jnp.where((own_token >= begin) & (own_token < end), begin, own_start)
        turn_start = jnp.where((turn_token >= begin) & (turn_token < end), begin, turn_start)
        begin = end
    prefix_rows[...] = prefix

    slot_ids = [2 * s, 2 * s + 1, 2 * s + 4 - 8 * zh, 2 * s + 5 - 8 * zh]
    slot_prefix = [jnp.int32(0)] * 4
    for i in range(32):
        held = table_ref[i]
        slot_prefix = [
            jnp.where(held == slot, jnp.int32(i // 8), p) for slot, p in zip(slot_ids, slot_prefix)
        ]

    inverse = jnp.exp((turn_lane & 63).astype(F32) * (-2.0 * math.log(THETA) / HEAD))
    angles = (2048 + turn_token - turn_start).astype(F32) * inverse
    lower = turn_lane < 64

    def spread(packed):
        other = pltpu.roll(packed, HEAD // 2, 1)
        return jnp.concatenate(
            [jnp.where(lower, packed, other), jnp.where(lower, other, packed)], axis=0
        )

    cosine, sine = spread(jnp.cos(angles)), spread(jnp.sin(angles))
    half_lane = lax.broadcasted_iota(jnp.int32, (TOK, HEAD), 1)
    sine = jnp.where(half_lane < HEAD // 2, -sine, sine)

    def head_rope(values, g):
        scaled = values * row_scale(values) * g
        return (scaled * cosine + pltpu.roll(scaled, HEAD // 2, 1) * sine).astype(BF16)

    loads[2].wait()
    q_raw = dot(normed[...], wq[...], 1, 0)
    q_all[mine] = head_rope(q_raw, q_gain_ref[...])
    q_copies = []

    def send_queries(n, block, dev):
        copy = remote(q_all.at[block], q_all.at[block], q_s.at[n], q_r.at[block], dev)
        copy.start()
        q_copies.append(copy)

    for n, (_, dev) in enumerate(y_peers):
        send_queries(n, mine, dev)

    loads[3].wait()
    pair = dot(normed[...], wkv[...], 1, 0).astype(BF16)
    key_rows = head_rope(pair[:, :HEAD].astype(F32), k_gain_ref[...])
    value_rows = pair[:, HEAD:]
    suf[2, 0] = key_rows
    suf[2, 1] = value_rows.T
    out_ref[1] = jnp.where(lax.rem(m, 2) == 0, key_rows, value_rows)

    suf_copy = remote(suf.at[2], suf.at[0], suf_s.at[0], suf_r.at[0], after)
    suf_copy.start()

    @pl.when(c == 0)
    def _():
        pl.semaphore_wait(ready, 1)
        remote(suf.at[2], suf.at[1], suf_s.at[1], suf_r.at[1], mate).start()

    send_queries(3, mine, mate)
    for n, (block, dev) in enumerate(y_peers):
        remote(q_all.at[block], q_all.at[block], q_s.at[0], q_r.at[block], dev).wait_recv()
        send_queries(4 + n, block, mate)

    pass_copies = []
    for b, ref in enumerate((kk, vt)):
        kv_copies[b].wait_recv()
        copy = remote(ref.at[2 + px], ref.at[2 + px], kx_s.at[b], kx_r.at[b], x_partner)
        copy.start()
        pass_copies.append(copy)

    def attend(core, first, keys):
        return slot_part(
            keys,
            [vt[first + b] for b in range(2)],
            q_all[pl.ds(core * 4, 4)].reshape(512, HEAD),
            [prefix_rows[pl.ds(core, 1), :] == slot_prefix[first + b] for b in range(2)],
        )

    own_keys = [cache_ref[pl.ds(b * 256, 256), pl.ds(0, HEAD)] for b in range(2)]

    def q_arrived(core):
        for k in range(4):
            block = core * 4 + k
            remote(q_all.at[block], q_all.at[block], q_s.at[0], q_r.at[block], mate).wait_recv()

    for core in range(2):
        pl.when(c != core)(functools.partial(q_arrived, core))
        peak, total, out = attend(core, 0, own_keys)
        half_stat[core, pl.ds(0, 1), :] = peak
        half_stat[core, pl.ds(1, 1), :] = total
        half_out[core] = out

    for copy in pass_copies:
        copy.wait_recv()
    suf_copy.wait_recv()

    @pl.when(c == 1)
    def _():
        remote(suf.at[0], suf.at[1], suf_s.at[1], suf_r.at[1], mate).start()

    def send_back(k, core):
        yy = lax.rem(y + k, 4)
        block, dev = core * 4 + yy, at_seq(yy * 4 + zh * 2 + core)
        remote(res_out.at[block], back_out.at[mine], o_s.at[block], o_r.at[mine], dev).start()
        remote(res_stat.at[block], back_stat.at[mine], st_s.at[block], st_r.at[mine], dev).start()

    for core in range(2):
        peak1, total1, out1 = attend(core, 2, [kk[2], kk[3]])
        peak0 = half_stat[core, pl.ds(0, 1), :]
        total0 = half_stat[core, pl.ds(1, 1), :]
        peak = jnp.maximum(peak0, peak1)
        f0, f1 = jnp.exp2(peak0 - peak), jnp.exp2(peak1 - peak)
        total = total0 * f0 + total1 * f1
        inverse = 1.0 / jnp.maximum(total, 1.0)
        out = (half_out[core] * (f0 * inverse) + out1 * (f1 * inverse)).astype(BF16)
        for yy in range(4):
            cols = slice(yy * TOK, (yy + 1) * TOK)
            res_out[core * 4 + yy] = out[:, cols]
            res_stat[core * 4 + yy, pl.ds(0, 1), :] = peak[:, cols]
            res_stat[core * 4 + yy, pl.ds(1, 1), :] = total[:, cols]
        for k in (2, 1, 3):
            send_back(k, core)
        pl.when(c != core)(functools.partial(send_back, 0, core))

    remote(suf.at[0], suf.at[1], suf_s.at[1], suf_r.at[1], mate).wait_recv()
    queries = q_all[mine]
    suffix_scores = []
    for k in range(3):
        at = (s - 2 + k) * TOK + lax.broadcasted_iota(jnp.int32, (TOK, TOK), 0)
        seen = (at >= own_start) & (at <= own_token)
        suffix_scores.append(
            jnp.where(seen, dot(suf[k, 0], queries, 1, 1) * SCALE, FLOOR)
        )
    suffix_peak = jnp.max(
        jnp.maximum(jnp.maximum(suffix_scores[0], suffix_scores[1]), suffix_scores[2]),
        axis=0,
        keepdims=True,
    )
    suffix_total = jnp.zeros((1, TOK), F32)
    suffix_out = jnp.zeros((HEAD, TOK), F32)
    for k in range(3):
        weight = jnp.exp2(suffix_scores[k] - suffix_peak)
        suffix_total += jnp.sum(weight, axis=0, keepdims=True)
        suffix_out += dot(suf[k, 1], weight.astype(BF16), 1, 0)

    parts = [(suffix_peak, suffix_total, suffix_out / suffix_total)]
    parts.append((res_stat[mine, pl.ds(0, 1), :], res_stat[mine, pl.ds(1, 1), :], res_out[mine]))
    for block, dev in yc_peers:
        remote(res_out.at[block], back_out.at[block], o_s.at[block], o_r.at[block], dev).wait_recv()
        remote(
            res_stat.at[block], back_stat.at[block], st_s.at[block], st_r.at[block], dev
        ).wait_recv()
        parts.append(
            (back_stat[block, pl.ds(0, 1), :], back_stat[block, pl.ds(1, 1), :], back_out[block])
        )
    best = parts[0][0]
    for peak, _, _ in parts[1:]:
        best = jnp.maximum(best, peak)
    weight_sum, accumulated = None, None
    for peak, total, out in parts:
        factor = total * jnp.exp2(peak - best)
        term = factor * out.astype(F32)
        weight_sum = factor if weight_sum is None else weight_sum + factor
        accumulated = term if accumulated is None else accumulated + term
    attended = (accumulated / weight_sum).astype(BF16)
    attended = attended.T

    z_rows = [zl, zl + 1 - 2 * lax.rem(zl, 2), lax.rem(zl + 2, 4), 3 - zl]
    def reduce_scatter(left, weight, blocks, from_x, from_z, to_z, xs, xr, zs, zr):
        sends = []
        for i in (3, 2, 1, 0):
            zz = z_rows[i]
            prod = dot(left, weight[:, pl.ds(pl.multiple_of(zz * 512, 512), 512)], 1, 0)
            prod = prod.astype(BF16)
            for k in range(4):
                blocks[i, k] = prod[:, k * HEAD : (k + 1) * HEAD]
            for k, hop in enumerate(hops):
                copy = remote(
                    blocks.at[i, lax.rem(x + hop, 4)],
                    from_x.at[i, k],
                    xs.at[i, k],
                    xr.at[i, k],
                    x_peers[k],
                )
                copy.start()
                sends.append(copy)
        z_sends = []
        for n, i in enumerate((3, 2, 1, 0)):
            for k in range(3):
                sends[n * 3 + k].wait_recv()
            acc = blocks[i, x].astype(F32)
            for k in range(3):
                acc = acc + from_x[i, k].astype(F32)
            if i:
                to_z[n] = acc.astype(BF16)
                copy = remote(to_z.at[n], from_z.at[n], zs.at[n], zr.at[n], at_mp(z_rows[i] * 4 + x))
                copy.start()
                z_sends.append(copy)
        for n, copy in enumerate(z_sends):
            copy.wait_recv()
            acc = acc + from_z[n].astype(F32)
        return acc, sends + z_sends

    loads[4].wait()
    summed, sends1 = reduce_scatter(
        attended, wo, part, part_x, part_z, sent_z, x_s, x_r, z_s, z_r
    )
    columns = pl.ds(pl.multiple_of(m * HEAD, HEAD), HEAD)
    residual = (hidden[:, columns].astype(F32) + summed).astype(BF16)

    gathered[m] = residual
    g_copies = []

    def share(block, dev):
        n = len(g_copies)
        copy = remote(gathered.at[block], gathered.at[block], g_s.at[n], g_r.at[block], dev)
        copy.start()
        g_copies.append(copy)

    def arrived(block):
        remote(
            gathered.at[block], gathered.at[block], g_s.at[0], g_r.at[block], z_peers[0]
        ).wait_recv()

    for i in (3, 2, 1):
        share(m, at_mp(z_rows[i] * 4 + x))
    for dev in x_peers:
        share(m, dev)
    for i in (1, 2, 3):
        arrived(z_rows[i] * 4 + x)
        for dev in x_peers:
            share(z_rows[i] * 4 + x, dev)
    for k in (5, 6, 7):
        loads[k].wait()
    square = jnp.zeros((TOK, HEAD), F32)
    gate, up = None, None
    for i in range(4):
        for hop in (1, 3, 2):
            arrived(z_rows[i] * 4 + lax.rem(x + hop, 4))
        base = z_rows[i] * 4
        scaled = []
        for k in range(4):
            v = gathered[base + k].astype(F32)
            square = square + v * v
            cols = pl.ds(pl.multiple_of((base + k) * HEAD, HEAD), HEAD)
            scaled.append((v * post_gain[:, cols]).astype(BF16))
        scaled = jnp.concatenate(scaled, axis=1)
        rows = pl.ds(pl.multiple_of(base * HEAD, 4 * HEAD), 4 * HEAD)
        gate_part, up_part = dot(scaled, wg[rows, :], 1, 0), dot(scaled, wu[rows, :], 1, 0)
        gate = gate_part if gate is None else gate + gate_part
        up = up_part if up is None else up + up_part
    scale = lax.rsqrt(jnp.sum(square, axis=-1, keepdims=True) * (1.0 / 2048) + EPSILON)
    gate, up = gate * scale, up * scale
    middle = (gate / (1.0 + jnp.exp(-gate)) * up).astype(BF16)
    loads[8].wait()
    summed, sends2 = reduce_scatter(
        middle, wd, part2, part2_x, part2_z, sent2_z, x2_s, x2_r, z2_s, z2_r
    )
    out_ref[0] = (residual.astype(F32) + summed).astype(BF16)

    remote(suf.at[2], suf.at[1], suf_s.at[1], suf_r.at[1], mate).wait_send()
    for copy in kv_copies + pass_copies + [suf_copy] + q_copies + sends1 + sends2 + g_copies:
        copy.wait_send()
    for block, dev in yc_peers:
        remote(res_out.at[block], back_out.at[block], o_s.at[block], o_r.at[block], dev).wait_send()
        remote(
            res_stat.at[block], back_stat.at[block], st_s.at[block], st_r.at[block], dev
        ).wait_send()


def local(
    hidden_in,
    input_gain,
    w_query,
    key_value_weight,
    query_gain,
    key_gain,
    w_out,
    post_gain,
    w_gate,
    w_up,
    w_down,
    prefix_slot_cache,
    block_table,
    request_prefix,
    suffix_lengths,
):
    my_model = lax.axis_index("mp")
    cache = lax.dynamic_slice_in_dim(prefix_slot_cache, lax.div(my_model, 2), 1, 2).reshape(512, 2 * HEAD)

    def in_hbm(value):
        return pltpu.with_memory_space_constraint(value, pltpu.HBM)

    vmem = pl.BlockSpec(memory_space=pltpu.VMEM)
    smem = pl.BlockSpec(memory_space=pltpu.SMEM)
    hbm = pl.BlockSpec(memory_space=pl.ANY)
    V = pltpu.VMEM
    D = pltpu.SemaphoreType.DMA
    block = (TOK, HEAD)
    both = pl.pallas_call(
        kernel,
        out_shape=jax.ShapeDtypeStruct((2, TOK, HEAD), BF16),
        in_specs=[smem] * 3 + [hbm] * 3 + [vmem] * 3 + [hbm] * 6,
        out_specs=vmem,
        scratch_shapes=[
            V((128, 2048), BF16),
            V((1, 2048), F32),
            V((1, 2048), F32),
            V((2048, 128), BF16),
            V((2048, 256), BF16),
            V((128, 2048), BF16),
            V((2048, 384), BF16),
            V((2048, 384), BF16),
            V((384, 2048), BF16),
            V((128, 2048), BF16),
            V((4, 256, 128), BF16),
            V((4, 128, 256), BF16),
            V((8,) + block, BF16),
            V((3, 2) + block, BF16),
            V((2, 128, 512), F32),
            V((2, 8, 512), F32),
            V((8,) + block, BF16),
            V((8, 8, 128), F32),
            V((8,) + block, BF16),
            V((8, 8, 128), F32),
            V((8, 512), jnp.int32),
            V((4, 4) + block, BF16),
            V((4, 3) + block, BF16),
            V((3,) + block, BF16),
            V((3,) + block, BF16),
            V((4, 4) + block, BF16),
            V((4, 3) + block, BF16),
            V((3,) + block, BF16),
            V((3,) + block, BF16),
            V((16,) + block, BF16),
            D((9,)),
            D((2,)),
            D((2,)),
            D((2,)),
            D((2,)),
            D((2,)),
            D((2,)),
            D((7,)),
            D((8,)),
            D((8,)),
            D((8,)),
            D((8,)),
            D((8,)),
            D((4, 3)),
            D((4, 3)),
            D((3,)),
            D((3,)),
            D((4, 3)),
            D((4, 3)),
            D((3,)),
            D((3,)),
            D((15,)),
            D((16,)),
            pltpu.SemaphoreType.REGULAR,
        ],
        compiler_params=pltpu.CompilerParams(
            collective_id=0, has_side_effects=True, vmem_limit_bytes=48 * 1024 * 1024
        ),
        name="layer",
    )(
        block_table,
        request_prefix,
        suffix_lengths,
        in_hbm(hidden_in),
        in_hbm(input_gain.reshape(1, -1)),
        in_hbm(post_gain.reshape(1, -1)),
        query_gain.reshape(1, -1),
        key_gain.reshape(1, -1),
        cache,
        in_hbm(w_query),
        in_hbm(key_value_weight),
        in_hbm(w_out),
        in_hbm(w_gate),
        in_hbm(w_up),
        in_hbm(w_down),
    )

    return both[0], both[1]


def solution(mesh):
    in_specs = (
        P("seq", None),
        P(),
        P(None, "mp"),
        P(None, "mp"),
        P(),
        P(),
        P("mp", None),
        P(),
        P(None, "mp"),
        P(None, "mp"),
        P("mp", None),
        P("seq", None, None, None),
        P(),
        P(),
        P(),
    )
    out_specs = (P("seq", "mp"), P("seq", "mp"))
    return jax.shard_map(local, mesh=mesh, in_specs=in_specs, out_specs=out_specs, check_vma=False)
```

```python
import functools
import math

import jax
import jax.numpy as jnp
from jax import lax
from jax.experimental import pallas as pl
from jax.experimental.pallas import tpu as pltpu
from jax.sharding import PartitionSpec as P

MESH = pl.DeviceIdType.MESH
HEAD = 128
TOK = 128
SEQ = 16
EPSILON = 1e-06
THETA = 1000000.0
FLOOR = -1e30
SCALE = math.log2(math.e) / math.sqrt(HEAD)
F32 = jnp.float32
BF16 = jnp.bfloat16


def dot(a, b, ca, cb):
    return lax.dot_general(a, b, (((ca,), (cb,)), ((), ())), preferred_element_type=F32)


def remote(src, dst, ss, rs, dev):
    return pltpu.make_async_remote_copy(
        src_ref=src, dst_ref=dst, send_sem=ss, recv_sem=rs, device_id=dev, device_id_type=MESH
    )


def row_scale(values):
    return lax.rsqrt(jnp.mean(values * values, axis=-1, keepdims=True) + EPSILON)


def slot_part(keys, values_t, queries, visible):
    scores = [dot(k, queries, 1, 1) for k in keys]
    peaks = [
        jnp.where(v, jnp.max(s, axis=0, keepdims=True) * SCALE, FLOOR)
        for s, v in zip(scores, visible)
    ]
    peak = jnp.maximum(peaks[0], peaks[1])
    total, out = None, None
    for s, v, vt in zip(scores, visible, values_t):
        weight = jnp.exp2(s * SCALE - jnp.where(v, peak, 1e30))
        part = jnp.sum(weight, axis=0, keepdims=True)
        prod = dot(vt, weight.astype(BF16), 1, 0)
        total = part if total is None else total + part
        out = prod if out is None else out + prod
    return peak, total, out


def kernel(
    table_ref,
    request_prefix_ref,
    lengths_ref,
    hidden_hbm,
    gain_hbm,
    post_gain_hbm,
    q_gain_ref,
    k_gain_ref,
    cache_ref,
    wq_hbm,
    wkv_hbm,
    wo_hbm,
    wg_hbm,
    wu_hbm,
    wd_hbm,
    out_ref,
    hidden,
    gain,
    post_gain,
    wq,
    wkv,
    wo,
    wg,
    wu,
    wd,
    normed,
    kk,
    vt,
    q_all,
    suf,
    half_out,
    half_stat,
    res_out,
    res_stat,
    back_out,
    back_stat,
    prefix_rows,
    part,
    part_x,
    part_z,
    sent_z,
    part2,
    part2_x,
    part2_z,
    sent2_z,
    gathered,
    dma_sem,
    kv_s,
    kv_r,
    kx_s,
    kx_r,
    suf_s,
    suf_r,
    q_s,
    q_r,
    o_s,
    o_r,
    st_s,
    st_r,
    x_s,
    x_r,
    z_s,
    z_r,
    x2_s,
    x2_r,
    z2_s,
    z2_r,
    g_s,
    g_r,
    ready,
):
    s = lax.axis_index("seq")
    m = lax.axis_index("mp")
    y, zh, c = lax.div(s, 4), lax.rem(lax.div(s, 2), 2), lax.rem(s, 2)
    zl, x = lax.div(m, 4), lax.rem(m, 4)

    def at_seq(i):
        return {"seq": i}

    def at_mp(i):
        return {"mp": i}

    z_peer = at_seq(y * 4 + (1 - zh) * 2 + c)
    yc_peers = []
    for dy, dc in ((0, 1), (1, 0), (1, 1), (3, 0), (3, 1), (2, 0), (2, 1)):
        yy, cc = lax.rem(y + dy, 4), lax.rem(c + dc, 2)
        yc_peers.append((cc * 4 + yy, at_seq(yy * 4 + zh * 2 + cc)))
    mate = yc_peers[0][1]
    y_peers = [yc_peers[k] for k in (5, 1, 3)]
    mine = c * 4 + y
    px = lax.rem(x, 2)
    x_partner = at_mp(zl * 4 + x + 1 - 2 * px)
    after, before = at_seq(lax.rem(s + 2, SEQ)), at_seq(lax.rem(s + 14, SEQ))
    hops = (2, 1, 3)
    x_peers = [at_mp(zl * 4 + lax.rem(x + i, 4)) for i in hops]
    z_peers = [at_mp(lax.rem(zl + i, 4) * 4 + x) for i in hops]

    same = [z_peer, after, before] + x_peers + z_peers + [dev for _, dev in y_peers]
    barrier = pltpu.get_barrier_semaphore()
    for dev in same:
        pl.semaphore_signal(barrier, inc=1, device_id=dev, device_id_type=MESH)

    @pl.when(c == 0)
    def _():
        pl.semaphore_signal(barrier, inc=1, device_id=mate, device_id_type=MESH)

    loads = []
    for k, (src, dst) in enumerate(
        [
            (hidden_hbm, hidden),
            (gain_hbm, gain),
            (wq_hbm, wq),
            (wkv_hbm, wkv),
            (wo_hbm, wo),
            (post_gain_hbm, post_gain),
            (wg_hbm, wg),
            (wu_hbm, wu),
            (wd_hbm, wd),
        ]
    ):
        copy = pltpu.make_async_copy(src, dst, dma_sem.at[k])
        copy.start()
        loads.append(copy)

    def turn_values(slot):
        vt[slot] = cache_ref[pl.ds(pl.multiple_of(slot * 256, 256), 256), pl.ds(HEAD, HEAD)].T

    turn_values(px)
    pl.semaphore_wait(barrier, len(same) + c)

    @pl.when(c == 1)
    def _():
        pl.semaphore_signal(ready, inc=1, device_id=mate, device_id_type=MESH)

    px_rows = pl.ds(pl.multiple_of(px * 256, 256), 256)
    kv_copies = [
        remote(
            cache_ref.at[px_rows, pl.ds(0, HEAD)], kk.at[2 + px], kv_s.at[0], kv_r.at[0], z_peer
        ),
        remote(vt.at[px], vt.at[2 + px], kv_s.at[1], kv_r.at[1], z_peer),
    ]
    for copy in kv_copies:
        copy.start()
    turn_values(1 - px)

    loads[0].wait()
    loads[1].wait()
    raw = hidden[...].astype(F32)
    normed[...] = (raw * row_scale(raw) * gain[...]).astype(BF16)

    lane = lax.broadcasted_iota(jnp.int32, (8, 512), 1)
    core = lax.broadcasted_iota(jnp.int32, (8, 512), 0)
    block_at = lax.shift_right_logical(lane, 7) * 4 + zh * 2 + core
    token = block_at * TOK + (lane & 127)
    own_token = s * TOK + lax.broadcasted_iota(jnp.int32, (1, TOK), 1)
    turn_lane = lax.broadcasted_iota(jnp.int32, (64, TOK), 1)
    turn_token = s * TOK + lax.broadcasted_iota(jnp.int32, (64, TOK), 0) + (turn_lane & 64)
    turn_start = jnp.zeros((64, TOK), jnp.int32)
    prefix = jnp.zeros((8, 512), jnp.int32)
    own_start = jnp.zeros((1, TOK), jnp.int32)
    begin = jnp.int32(0)
    for r in range(32):
        end = begin + lengths_ref[r]
        prefix = jnp.where((token >= begin) & (token < end), request_prefix_ref[r], prefix)
        own_start = jnp.where((own_token >= begin) & (own_token < end), begin, own_start)
        turn_start = jnp.where((turn_token >= begin) & (turn_token < end), begin, turn_start)
        begin = end
    prefix_rows[...] = prefix

    slot_ids = [2 * s, 2 * s + 1, 2 * s + 4 - 8 * zh, 2 * s + 5 - 8 * zh]
    slot_prefix = [jnp.int32(0)] * 4
    for i in range(32):
        held = table_ref[i]
        slot_prefix = [
            jnp.where(held == slot, jnp.int32(i // 8), p) for slot, p in zip(slot_ids, slot_prefix)
        ]

    inverse = jnp.exp((turn_lane & 63).astype(F32) * (-2.0 * math.log(THETA) / HEAD))
    angles = (2048 + turn_token - turn_start).astype(F32) * inverse
    lower = turn_lane < 64

    def spread(packed):
        other = pltpu.roll(packed, HEAD // 2, 1)
        return jnp.concatenate(
            [jnp.where(lower, packed, other), jnp.where(lower, other, packed)], axis=0
        )

    cosine, sine = spread(jnp.cos(angles)), spread(jnp.sin(angles))
    half_lane = lax.broadcasted_iota(jnp.int32, (TOK, HEAD), 1)
    sine = jnp.where(half_lane < HEAD // 2, -sine, sine)

    def head_rope(values, g):
        scaled = values * row_scale(values) * g
        return (scaled * cosine + pltpu.roll(scaled, HEAD // 2, 1) * sine).astype(BF16)

    loads[2].wait()
    q_raw = dot(normed[...], wq[...], 1, 0)
    q_all[mine] = head_rope(q_raw, q_gain_ref[...])
    q_copies = []

    def send_queries(n, block, dev):
        copy = remote(q_all.at[block], q_all.at[block], q_s.at[n], q_r.at[block], dev)
        copy.start()
        q_copies.append(copy)

    for n, (_, dev) in enumerate(y_peers):
        send_queries(n, mine, dev)

    loads[3].wait()
    pair = dot(normed[...], wkv[...], 1, 0).astype(BF16)
    key_rows = head_rope(pair[:, :HEAD].astype(F32), k_gain_ref[...])
    value_rows = pair[:, HEAD:]
    suf[2, 0] = key_rows
    suf[2, 1] = value_rows.T
    out_ref[1] = jnp.where(lax.rem(m, 2) == 0, key_rows, value_rows)

    suf_copy = remote(suf.at[2], suf.at[0], suf_s.at[0], suf_r.at[0], after)
    suf_copy.start()

    @pl.when(c == 0)
    def _():
        pl.semaphore_wait(ready, 1)
        remote(suf.at[2], suf.at[1], suf_s.at[1], suf_r.at[1], mate).start()

    send_queries(3, mine, mate)
    for n, (block, dev) in enumerate(y_peers):
        remote(q_all.at[block], q_all.at[block], q_s.at[0], q_r.at[block], dev).wait_recv()
        send_queries(4 + n, block, mate)

    pass_copies = []
    for b, ref in enumerate((kk, vt)):
        kv_copies[b].wait_recv()
        copy = remote(ref.at[2 + px], ref.at[2 + px], kx_s.at[b], kx_r.at[b], x_partner)
        copy.start()
        pass_copies.append(copy)

    def attend(core, first, keys):
        return slot_part(
            keys,
            [vt[first + b] for b in range(2)],
            q_all[pl.ds(core * 4, 4)].reshape(512, HEAD),
            [prefix_rows[pl.ds(core, 1), :] == slot_prefix[first + b] for b in range(2)],
        )

    own_keys = [cache_ref[pl.ds(b * 256, 256), pl.ds(0, HEAD)] for b in range(2)]

    def q_arrived(core):
        for k in range(4):
            block = core * 4 + k
            remote(q_all.at[block], q_all.at[block], q_s.at[0], q_r.at[block], mate).wait_recv()

    for core in range(2):
        pl.when(c != core)(functools.partial(q_arrived, core))
        peak, total, out = attend(core, 0, own_keys)
        half_stat[core, pl.ds(0, 1), :] = peak
        half_stat[core, pl.ds(1, 1), :] = total
        half_out[core] = out

    suf_copy.wait_recv()

    @pl.when(c == 1)
    def _():
        remote(suf.at[0], suf.at[1], suf_s.at[1], suf_r.at[1], mate).start()

    for copy in pass_copies:
        copy.wait_recv()
    def send_back(k, core):
        yy = lax.rem(y + k, 4)
        block, dev = core * 4 + yy, at_seq(yy * 4 + zh * 2 + core)
        remote(res_out.at[block], back_out.at[mine], o_s.at[block], o_r.at[mine], dev).start()
        remote(res_stat.at[block], back_stat.at[mine], st_s.at[block], st_r.at[mine], dev).start()

    for core in range(2):
        peak1, total1, out1 = attend(core, 2, [kk[2], kk[3]])
        peak0 = half_stat[core, pl.ds(0, 1), :]
        total0 = half_stat[core, pl.ds(1, 1), :]
        peak = jnp.maximum(peak0, peak1)
        f0, f1 = jnp.exp2(peak0 - peak), jnp.exp2(peak1 - peak)
        total = total0 * f0 + total1 * f1
        inverse = 1.0 / jnp.maximum(total, 1.0)
        out = (half_out[core] * (f0 * inverse) + out1 * (f1 * inverse)).astype(BF16)
        for yy in range(4):
            cols = slice(yy * TOK, (yy + 1) * TOK)
            res_out[core * 4 + yy] = out[:, cols]
            res_stat[core * 4 + yy, pl.ds(0, 1), :] = peak[:, cols]
            res_stat[core * 4 + yy, pl.ds(1, 1), :] = total[:, cols]
        for k in (2, 1, 3):
            send_back(k, core)
        pl.when(c != core)(functools.partial(send_back, 0, core))

    remote(suf.at[0], suf.at[1], suf_s.at[1], suf_r.at[1], mate).wait_recv()
    queries = q_all[mine]
    suffix_scores = []
    for k in range(3):
        at = (s - 2 + k) * TOK + lax.broadcasted_iota(jnp.int32, (TOK, TOK), 0)
        seen = (at >= own_start) & (at <= own_token)
        suffix_scores.append(
            jnp.where(seen, dot(suf[k, 0], queries, 1, 1) * SCALE, FLOOR)
        )
    suffix_peak = jnp.max(
        jnp.maximum(jnp.maximum(suffix_scores[0], suffix_scores[1]), suffix_scores[2]),
        axis=0,
        keepdims=True,
    )
    suffix_total = jnp.zeros((1, TOK), F32)
    suffix_out = jnp.zeros((HEAD, TOK), F32)
    for k in range(3):
        weight = jnp.exp2(suffix_scores[k] - suffix_peak)
        suffix_total += jnp.sum(weight, axis=0, keepdims=True)
        suffix_out += dot(suf[k, 1], weight.astype(BF16), 1, 0)

    parts = [(suffix_peak, suffix_total, suffix_out / suffix_total)]
    parts.append((res_stat[mine, pl.ds(0, 1), :], res_stat[mine, pl.ds(1, 1), :], res_out[mine]))
    for block, dev in yc_peers:
        remote(res_out.at[block], back_out.at[block], o_s.at[block], o_r.at[block], dev).wait_recv()
        remote(
            res_stat.at[block], back_stat.at[block], st_s.at[block], st_r.at[block], dev
        ).wait_recv()
        parts.append(
            (back_stat[block, pl.ds(0, 1), :], back_stat[block, pl.ds(1, 1), :], back_out[block])
        )
    best = parts[0][0]
    for peak, _, _ in parts[1:]:
        best = jnp.maximum(best, peak)
    weight_sum, accumulated = None, None
    for peak, total, out in parts:
        factor = total * jnp.exp2(peak - best)
        term = factor * out.astype(F32)
        weight_sum = factor if weight_sum is None else weight_sum + factor
        accumulated = term if accumulated is None else accumulated + term
    attended = (accumulated / weight_sum).astype(BF16)
    attended = attended.T

    z_rows = [zl, zl + 1 - 2 * lax.rem(zl, 2), lax.rem(zl + 2, 4), 3 - zl]
    def drain_attention():
        remote(suf.at[2], suf.at[1], suf_s.at[1], suf_r.at[1], mate).wait_send()
        for copy in kv_copies + pass_copies + [suf_copy] + q_copies:
            copy.wait_send()
        for block, dev in yc_peers:
            remote(
                res_out.at[block], back_out.at[block], o_s.at[block], o_r.at[block], dev
            ).wait_send()
            remote(
                res_stat.at[block], back_stat.at[block], st_s.at[block], st_r.at[block], dev
            ).wait_send()

    def reduce_scatter(left, weight, blocks, from_x, from_z, to_z, xs, xr, zs, zr, meanwhile):
        sends = []
        for i in (3, 2, 1, 0):
            zz = z_rows[i]
            prod = dot(left, weight[:, pl.ds(pl.multiple_of(zz * 512, 512), 512)], 1, 0)
            prod = prod.astype(BF16)
            for k in range(4):
                blocks[i, k] = prod[:, k * HEAD : (k + 1) * HEAD]
            for k, hop in enumerate(hops):
                copy = remote(
                    blocks.at[i, lax.rem(x + hop, 4)],
                    from_x.at[i, k],
                    xs.at[i, k],
                    xr.at[i, k],
                    x_peers[k],
                )
                copy.start()
                sends.append(copy)
        meanwhile()
        z_sends = []
        for n, i in enumerate((3, 2, 1, 0)):
            for k in range(3):
                sends[n * 3 + k].wait_recv()
            acc = blocks[i, x].astype(F32)
            for k in range(3):
                acc = acc + from_x[i, k].astype(F32)
            if i:
                to_z[n] = acc.astype(BF16)
                copy = remote(to_z.at[n], from_z.at[n], zs.at[n], zr.at[n], at_mp(z_rows[i] * 4 + x))
                copy.start()
                z_sends.append(copy)
        for n, copy in enumerate(z_sends):
            copy.wait_recv()
            acc = acc + from_z[n].astype(F32)
        return acc, sends + z_sends

    loads[4].wait()
    summed, sends1 = reduce_scatter(
        attended, wo, part, part_x, part_z, sent_z, x_s, x_r, z_s, z_r, drain_attention
    )
    columns = pl.ds(pl.multiple_of(m * HEAD, HEAD), HEAD)
    residual = (hidden[:, columns].astype(F32) + summed).astype(BF16)

    gathered[m] = residual
    g_copies = []

    def share(block, dev):
        n = len(g_copies)
        copy = remote(gathered.at[block], gathered.at[block], g_s.at[n], g_r.at[block], dev)
        copy.start()
        g_copies.append(copy)

    def arrived(block):
        remote(
            gathered.at[block], gathered.at[block], g_s.at[0], g_r.at[block], z_peers[0]
        ).wait_recv()

    for i in (3, 2, 1):
        share(m, at_mp(z_rows[i] * 4 + x))
    for dev in x_peers:
        share(m, dev)
    for i in (1, 2, 3):
        arrived(z_rows[i] * 4 + x)
        for dev in x_peers:
            share(z_rows[i] * 4 + x, dev)
    for k in (5, 6, 7):
        loads[k].wait()
    square = jnp.zeros((TOK, HEAD), F32)
    gate, up = None, None
    for i in range(4):
        for hop in (1, 3, 2):
            arrived(z_rows[i] * 4 + lax.rem(x + hop, 4))
        base = z_rows[i] * 4
        scaled = []
        for k in range(4):
            v = gathered[base + k].astype(F32)
            square = square + v * v
            cols = pl.ds(pl.multiple_of((base + k) * HEAD, HEAD), HEAD)
            scaled.append((v * post_gain[:, cols]).astype(BF16))
        scaled = jnp.concatenate(scaled, axis=1)
        rows = pl.ds(pl.multiple_of(base * HEAD, 4 * HEAD), 4 * HEAD)
        gate_part, up_part = dot(scaled, wg[rows, :], 1, 0), dot(scaled, wu[rows, :], 1, 0)
        gate = gate_part if gate is None else gate + gate_part
        up = up_part if up is None else up + up_part
    scale = lax.rsqrt(jnp.sum(square, axis=-1, keepdims=True) * (1.0 / 2048) + EPSILON)
    gate, up = gate * scale, up * scale
    middle = (gate / (1.0 + jnp.exp(-gate)) * up).astype(BF16)

    def drain_residual():
        for copy in sends1 + g_copies:
            copy.wait_send()

    loads[8].wait()
    summed, sends2 = reduce_scatter(
        middle, wd, part2, part2_x, part2_z, sent2_z, x2_s, x2_r, z2_s, z2_r, drain_residual
    )
    out_ref[0] = (residual.astype(F32) + summed).astype(BF16)

    for copy in sends2:
        copy.wait_send()


def local(
    hidden_in,
    input_gain,
    w_query,
    key_value_weight,
    query_gain,
    key_gain,
    w_out,
    post_gain,
    w_gate,
    w_up,
    w_down,
    prefix_slot_cache,
    block_table,
    request_prefix,
    suffix_lengths,
):
    my_model = lax.axis_index("mp")
    cache = lax.dynamic_slice_in_dim(prefix_slot_cache, lax.div(my_model, 2), 1, 2).reshape(512, 2 * HEAD)

    def in_hbm(value):
        return pltpu.with_memory_space_constraint(value, pltpu.HBM)

    vmem = pl.BlockSpec(memory_space=pltpu.VMEM)
    smem = pl.BlockSpec(memory_space=pltpu.SMEM)
    hbm = pl.BlockSpec(memory_space=pl.ANY)
    V = pltpu.VMEM
    D = pltpu.SemaphoreType.DMA
    block = (TOK, HEAD)
    both = pl.pallas_call(
        kernel,
        out_shape=jax.ShapeDtypeStruct((2, TOK, HEAD), BF16),
        in_specs=[smem] * 3 + [hbm] * 3 + [vmem] * 3 + [hbm] * 6,
        out_specs=vmem,
        scratch_shapes=[
            V((128, 2048), BF16),
            V((1, 2048), F32),
            V((1, 2048), F32),
            V((2048, 128), BF16),
            V((2048, 256), BF16),
            V((128, 2048), BF16),
            V((2048, 384), BF16),
            V((2048, 384), BF16),
            V((384, 2048), BF16),
            V((128, 2048), BF16),
            V((4, 256, 128), BF16),
            V((4, 128, 256), BF16),
            V((8,) + block, BF16),
            V((3, 2) + block, BF16),
            V((2, 128, 512), F32),
            V((2, 8, 512), F32),
            V((8,) + block, BF16),
            V((8, 8, 128), F32),
            V((8,) + block, BF16),
            V((8, 8, 128), F32),
            V((8, 512), jnp.int32),
            V((4, 4) + block, BF16),
            V((4, 3) + block, BF16),
            V((3,) + block, BF16),
            V((3,) + block, BF16),
            V((4, 4) + block, BF16),
            V((4, 3) + block, BF16),
            V((3,) + block, BF16),
            V((3,) + block, BF16),
            V((16,) + block, BF16),
            D((9,)),
            D((2,)),
            D((2,)),
            D((2,)),
            D((2,)),
            D((2,)),
            D((2,)),
            D((7,)),
            D((8,)),
            D((8,)),
            D((8,)),
            D((8,)),
            D((8,)),
            D((4, 3)),
            D((4, 3)),
            D((3,)),
            D((3,)),
            D((4, 3)),
            D((4, 3)),
            D((3,)),
            D((3,)),
            D((15,)),
            D((16,)),
            pltpu.SemaphoreType.REGULAR,
        ],
        compiler_params=pltpu.CompilerParams(
            collective_id=0, has_side_effects=True, vmem_limit_bytes=48 * 1024 * 1024
        ),
        name="layer",
    )(
        block_table,
        request_prefix,
        suffix_lengths,
        in_hbm(hidden_in),
        in_hbm(input_gain.reshape(1, -1)),
        in_hbm(post_gain.reshape(1, -1)),
        query_gain.reshape(1, -1),
        key_gain.reshape(1, -1),
        cache,
        in_hbm(w_query),
        in_hbm(key_value_weight),
        in_hbm(w_out),
        in_hbm(w_gate),
        in_hbm(w_up),
        in_hbm(w_down),
    )

    return both[0], both[1]


def solution(mesh):
    in_specs = (
        P("seq", None),
        P(),
        P(None, "mp"),
        P(None, "mp"),
        P(),
        P(),
        P("mp", None),
        P(),
        P(None, "mp"),
        P(None, "mp"),
        P("mp", None),
        P("seq", None, None, None),
        P(),
        P(),
        P(),
    )
    out_specs = (P("seq", "mp"), P("seq", "mp"))
    return jax.shard_map(local, mesh=mesh, in_specs=in_specs, out_specs=out_specs, check_vma=False)
```

```python
import functools
import math

import jax
import jax.numpy as jnp
from jax import lax
from jax.experimental import pallas as pl
from jax.experimental.pallas import tpu as pltpu
from jax.sharding import PartitionSpec as P

MESH = pl.DeviceIdType.MESH
HEAD = 128
TOK = 128
SEQ = 16
EPSILON = 1e-06
THETA = 1000000.0
FLOOR = -1e30
SCALE = math.log2(math.e) / math.sqrt(HEAD)
F32 = jnp.float32
BF16 = jnp.bfloat16


def dot(a, b, ca, cb):
    return lax.dot_general(a, b, (((ca,), (cb,)), ((), ())), preferred_element_type=F32)


def remote(src, dst, ss, rs, dev):
    return pltpu.make_async_remote_copy(
        src_ref=src, dst_ref=dst, send_sem=ss, recv_sem=rs, device_id=dev, device_id_type=MESH
    )


def row_scale(values):
    return lax.rsqrt(jnp.mean(values * values, axis=-1, keepdims=True) + EPSILON)


def slot_part(keys, values_t, queries, visible):
    scores = [dot(k, queries, 1, 1) for k in keys]
    peaks = [
        jnp.where(v, jnp.max(s, axis=0, keepdims=True) * SCALE, FLOOR)
        for s, v in zip(scores, visible)
    ]
    peak = jnp.maximum(peaks[0], peaks[1])
    total, out = None, None
    for s, v, vt in zip(scores, visible, values_t):
        weight = jnp.exp2(s * SCALE - jnp.where(v, peak, 1e30))
        part = jnp.sum(weight, axis=0, keepdims=True)
        prod = dot(vt, weight.astype(BF16), 1, 0)
        total = part if total is None else total + part
        out = prod if out is None else out + prod
    return peak, total, out


def kernel(
    table_ref,
    request_prefix_ref,
    lengths_ref,
    hidden_hbm,
    gain_hbm,
    post_gain_hbm,
    q_gain_ref,
    k_gain_ref,
    cache_ref,
    wq_hbm,
    wkv_hbm,
    wo_hbm,
    wg_hbm,
    wu_hbm,
    wd_hbm,
    out_ref,
    hidden,
    gain,
    post_gain,
    wq,
    wkv,
    wo,
    wg,
    wu,
    wd,
    normed,
    kk,
    vt,
    q_all,
    suf,
    half_out,
    half_stat,
    res_out,
    res_stat,
    back_out,
    back_stat,
    prefix_rows,
    part,
    part_x,
    part_z,
    sent_z,
    part2,
    part2_x,
    part2_z,
    sent2_z,
    gathered,
    dma_sem,
    kv_s,
    kv_r,
    kx_s,
    kx_r,
    suf_s,
    suf_r,
    q_s,
    q_r,
    o_s,
    o_r,
    st_s,
    st_r,
    x_s,
    x_r,
    z_s,
    z_r,
    x2_s,
    x2_r,
    z2_s,
    z2_r,
    g_s,
    g_r,
    ready,
):
    s = lax.axis_index("seq")
    m = lax.axis_index("mp")
    y, zh, c = lax.div(s, 4), lax.rem(lax.div(s, 2), 2), lax.rem(s, 2)
    zl, x = lax.div(m, 4), lax.rem(m, 4)

    def at_seq(i):
        return {"seq": i}

    def at_mp(i):
        return {"mp": i}

    z_peer = at_seq(y * 4 + (1 - zh) * 2 + c)
    yc_peers = []
    for dy, dc in ((0, 1), (1, 0), (1, 1), (3, 0), (3, 1), (2, 0), (2, 1)):
        yy, cc = lax.rem(y + dy, 4), lax.rem(c + dc, 2)
        yc_peers.append((cc * 4 + yy, at_seq(yy * 4 + zh * 2 + cc)))
    mate = yc_peers[0][1]
    y_peers = [yc_peers[k] for k in (5, 1, 3)]
    mine = c * 4 + y
    px = lax.rem(x, 2)
    x_partner = at_mp(zl * 4 + x + 1 - 2 * px)
    after, before = at_seq(lax.rem(s + 2, SEQ)), at_seq(lax.rem(s + 14, SEQ))
    hops = (2, 1, 3)
    x_peers = [at_mp(zl * 4 + lax.rem(x + i, 4)) for i in hops]
    z_peers = [at_mp(lax.rem(zl + i, 4) * 4 + x) for i in hops]

    same = [z_peer, after, before] + x_peers + z_peers + [dev for _, dev in y_peers]
    barrier = pltpu.get_barrier_semaphore()
    for dev in same:
        pl.semaphore_signal(barrier, inc=1, device_id=dev, device_id_type=MESH)

    @pl.when(c == 0)
    def _():
        pl.semaphore_signal(barrier, inc=1, device_id=mate, device_id_type=MESH)

    loads = []
    for k, (src, dst) in enumerate(
        [
            (hidden_hbm, hidden),
            (gain_hbm, gain),
            (wq_hbm, wq),
            (wkv_hbm, wkv),
            (wo_hbm, wo),
            (post_gain_hbm, post_gain),
            (wg_hbm, wg),
            (wu_hbm, wu),
            (wd_hbm, wd),
        ]
    ):
        copy = pltpu.make_async_copy(src, dst, dma_sem.at[k])
        copy.start()
        loads.append(copy)

    def turn_values(slot):
        vt[slot] = cache_ref[pl.ds(pl.multiple_of(slot * 256, 256), 256), pl.ds(HEAD, HEAD)].T

    turn_values(px)
    pl.semaphore_wait(barrier, len(same) + c)

    @pl.when(c == 1)
    def _():
        pl.semaphore_signal(ready, inc=1, device_id=mate, device_id_type=MESH)

    px_rows = pl.ds(pl.multiple_of(px * 256, 256), 256)
    kv_copies = [
        remote(
            cache_ref.at[px_rows, pl.ds(0, HEAD)], kk.at[2 + px], kv_s.at[0], kv_r.at[0], z_peer
        ),
        remote(vt.at[px], vt.at[2 + px], kv_s.at[1], kv_r.at[1], z_peer),
    ]
    for copy in kv_copies:
        copy.start()
    turn_values(1 - px)

    loads[0].wait()
    loads[1].wait()
    raw = hidden[...].astype(F32)
    normed[...] = (raw * row_scale(raw) * gain[...]).astype(BF16)

    lane = lax.broadcasted_iota(jnp.int32, (8, 512), 1)
    core = lax.broadcasted_iota(jnp.int32, (8, 512), 0)
    block_at = lax.shift_right_logical(lane, 7) * 4 + zh * 2 + core
    token = block_at * TOK + (lane & 127)
    own_token = s * TOK + lax.broadcasted_iota(jnp.int32, (1, TOK), 1)
    turn_lane = lax.broadcasted_iota(jnp.int32, (64, TOK), 1)
    turn_token = s * TOK + lax.broadcasted_iota(jnp.int32, (64, TOK), 0) + (turn_lane & 64)
    turn_start = jnp.zeros((64, TOK), jnp.int32)
    prefix = jnp.zeros((8, 512), jnp.int32)
    own_start = jnp.zeros((1, TOK), jnp.int32)
    begin = jnp.int32(0)
    for r in range(32):
        end = begin + lengths_ref[r]
        prefix = jnp.where((token >= begin) & (token < end), request_prefix_ref[r], prefix)
        own_start = jnp.where((own_token >= begin) & (own_token < end), begin, own_start)
        turn_start = jnp.where((turn_token >= begin) & (turn_token < end), begin, turn_start)
        begin = end
    prefix_rows[...] = prefix

    slot_ids = [2 * s, 2 * s + 1, 2 * s + 4 - 8 * zh, 2 * s + 5 - 8 * zh]
    slot_prefix = [jnp.int32(0)] * 4
    for i in range(32):
        held = table_ref[i]
        slot_prefix = [
            jnp.where(held == slot, jnp.int32(i // 8), p) for slot, p in zip(slot_ids, slot_prefix)
        ]

    inverse = jnp.exp((turn_lane & 63).astype(F32) * (-2.0 * math.log(THETA) / HEAD))
    angles = (2048 + turn_token - turn_start).astype(F32) * inverse
    lower = turn_lane < 64

    def spread(packed):
        other = pltpu.roll(packed, HEAD // 2, 1)
        return jnp.concatenate(
            [jnp.where(lower, packed, other), jnp.where(lower, other, packed)], axis=0
        )

    cosine, sine = spread(jnp.cos(angles)), spread(jnp.sin(angles))
    half_lane = lax.broadcasted_iota(jnp.int32, (TOK, HEAD), 1)
    sine = jnp.where(half_lane < HEAD // 2, -sine, sine)

    def head_rope(values, g):
        scaled = values * row_scale(values) * g
        return (scaled * cosine + pltpu.roll(scaled, HEAD // 2, 1) * sine).astype(BF16)

    loads[2].wait()
    q_raw = dot(normed[...], wq[...], 1, 0)
    q_all[mine] = head_rope(q_raw, q_gain_ref[...])
    q_copies = []

    def send_queries(n, block, dev):
        copy = remote(q_all.at[block], q_all.at[block], q_s.at[n], q_r.at[block], dev)
        copy.start()
        q_copies.append(copy)

    for n, (_, dev) in enumerate(y_peers):
        send_queries(n, mine, dev)

    loads[3].wait()
    pair = dot(normed[...], wkv[...], 1, 0).astype(BF16)
    key_rows = head_rope(pair[:, :HEAD].astype(F32), k_gain_ref[...])
    value_rows = pair[:, HEAD:]
    suf[2, 0] = key_rows
    suf[2, 1] = value_rows.T
    out_ref[1] = jnp.where(lax.rem(m, 2) == 0, key_rows, value_rows)

    suf_copy = remote(suf.at[2], suf.at[0], suf_s.at[0], suf_r.at[0], after)
    suf_copy.start()

    @pl.when(c == 0)
    def _():
        pl.semaphore_wait(ready, 1)
        remote(suf.at[2], suf.at[1], suf_s.at[1], suf_r.at[1], mate).start()

    send_queries(3, mine, mate)
    pass_copies = []

    def pass_on(b, ref):
        kv_copies[b].wait_recv()
        copy = remote(ref.at[2 + px], ref.at[2 + px], kx_s.at[b], kx_r.at[b], x_partner)
        copy.start()
        pass_copies.append(copy)

    pass_on(0, kk)
    for n, (block, dev) in enumerate(y_peers):
        remote(q_all.at[block], q_all.at[block], q_s.at[0], q_r.at[block], dev).wait_recv()
        send_queries(4 + n, block, mate)

    pass_on(1, vt)

    def attend(core, first, keys):
        return slot_part(
            keys,
            [vt[first + b] for b in range(2)],
            q_all[pl.ds(core * 4, 4)].reshape(512, HEAD),
            [prefix_rows[pl.ds(core, 1), :] == slot_prefix[first + b] for b in range(2)],
        )

    own_keys = [cache_ref[pl.ds(b * 256, 256), pl.ds(0, HEAD)] for b in range(2)]

    def q_arrived(core):
        for k in range(4):
            block = core * 4 + k
            remote(q_all.at[block], q_all.at[block], q_s.at[0], q_r.at[block], mate).wait_recv()

    for core in range(2):
        pl.when(c != core)(functools.partial(q_arrived, core))
        peak, total, out = attend(core, 0, own_keys)
        half_stat[core, pl.ds(0, 1), :] = peak
        half_stat[core, pl.ds(1, 1), :] = total
        half_out[core] = out

    suf_copy.wait_recv()

    @pl.when(c == 1)
    def _():
        remote(suf.at[0], suf.at[1], suf_s.at[1], suf_r.at[1], mate).start()

    for copy in pass_copies:
        copy.wait_recv()
    def send_back(k, core):
        yy = lax.rem(y + k, 4)
        block, dev = core * 4 + yy, at_seq(yy * 4 + zh * 2 + core)
        remote(res_out.at[block], back_out.at[mine], o_s.at[block], o_r.at[mine], dev).start()
        remote(res_stat.at[block], back_stat.at[mine], st_s.at[block], st_r.at[mine], dev).start()

    for core in range(2):
        peak1, total1, out1 = attend(core, 2, [kk[2], kk[3]])
        peak0 = half_stat[core, pl.ds(0, 1), :]
        total0 = half_stat[core, pl.ds(1, 1), :]
        peak = jnp.maximum(peak0, peak1)
        f0, f1 = jnp.exp2(peak0 - peak), jnp.exp2(peak1 - peak)
        total = total0 * f0 + total1 * f1
        inverse = 1.0 / jnp.maximum(total, 1.0)
        out = (half_out[core] * (f0 * inverse) + out1 * (f1 * inverse)).astype(BF16)
        for yy in range(4):
            cols = slice(yy * TOK, (yy + 1) * TOK)
            res_out[core * 4 + yy] = out[:, cols]
            res_stat[core * 4 + yy, pl.ds(0, 1), :] = peak[:, cols]
            res_stat[core * 4 + yy, pl.ds(1, 1), :] = total[:, cols]
        for k in (2, 1, 3):
            send_back(k, core)
        pl.when(c != core)(functools.partial(send_back, 0, core))

    remote(suf.at[0], suf.at[1], suf_s.at[1], suf_r.at[1], mate).wait_recv()
    queries = q_all[mine]
    suffix_scores = []
    for k in range(3):
        at = (s - 2 + k) * TOK + lax.broadcasted_iota(jnp.int32, (TOK, TOK), 0)
        seen = (at >= own_start) & (at <= own_token)
        suffix_scores.append(
            jnp.where(seen, dot(suf[k, 0], queries, 1, 1) * SCALE, FLOOR)
        )
    suffix_peak = jnp.max(
        jnp.maximum(jnp.maximum(suffix_scores[0], suffix_scores[1]), suffix_scores[2]),
        axis=0,
        keepdims=True,
    )
    suffix_total = jnp.zeros((1, TOK), F32)
    suffix_out = jnp.zeros((HEAD, TOK), F32)
    for k in range(3):
        weight = jnp.exp2(suffix_scores[k] - suffix_peak)
        suffix_total += jnp.sum(weight, axis=0, keepdims=True)
        suffix_out += dot(suf[k, 1], weight.astype(BF16), 1, 0)

    parts = [(suffix_peak, suffix_total, suffix_out / suffix_total)]
    parts.append((res_stat[mine, pl.ds(0, 1), :], res_stat[mine, pl.ds(1, 1), :], res_out[mine]))
    for block, dev in yc_peers:
        remote(res_out.at[block], back_out.at[block], o_s.at[block], o_r.at[block], dev).wait_recv()
        remote(
            res_stat.at[block], back_stat.at[block], st_s.at[block], st_r.at[block], dev
        ).wait_recv()
        parts.append(
            (back_stat[block, pl.ds(0, 1), :], back_stat[block, pl.ds(1, 1), :], back_out[block])
        )
    best = parts[0][0]
    for peak, _, _ in parts[1:]:
        best = jnp.maximum(best, peak)
    weight_sum, accumulated = None, None
    for peak, total, out in parts:
        factor = total * jnp.exp2(peak - best)
        term = factor * out.astype(F32)
        weight_sum = factor if weight_sum is None else weight_sum + factor
        accumulated = term if accumulated is None else accumulated + term
    attended = (accumulated / weight_sum).astype(BF16)
    attended = attended.T

    z_rows = [zl, zl + 1 - 2 * lax.rem(zl, 2), lax.rem(zl + 2, 4), 3 - zl]
    def drain_attention():
        remote(suf.at[2], suf.at[1], suf_s.at[1], suf_r.at[1], mate).wait_send()
        for copy in kv_copies + pass_copies + [suf_copy] + q_copies:
            copy.wait_send()
        for block, dev in yc_peers:
            remote(
                res_out.at[block], back_out.at[block], o_s.at[block], o_r.at[block], dev
            ).wait_send()
            remote(
                res_stat.at[block], back_stat.at[block], st_s.at[block], st_r.at[block], dev
            ).wait_send()

    def reduce_scatter(left, weight, blocks, from_x, from_z, to_z, xs, xr, zs, zr, meanwhile):
        sends = []
        for i in (3, 2, 1, 0):
            zz = z_rows[i]
            prod = dot(left, weight[:, pl.ds(pl.multiple_of(zz * 512, 512), 512)], 1, 0)
            prod = prod.astype(BF16)
            for k in range(4):
                blocks[i, k] = prod[:, k * HEAD : (k + 1) * HEAD]
            for k, hop in enumerate(hops):
                copy = remote(
                    blocks.at[i, lax.rem(x + hop, 4)],
                    from_x.at[i, k],
                    xs.at[i, k],
                    xr.at[i, k],
                    x_peers[k],
                )
                copy.start()
                sends.append(copy)
        meanwhile()
        z_sends = []
        for n, i in enumerate((3, 2, 1, 0)):
            for k in range(3):
                sends[n * 3 + k].wait_recv()
            acc = blocks[i, x].astype(F32)
            for k in range(3):
                acc = acc + from_x[i, k].astype(F32)
            if i:
                to_z[n] = acc.astype(BF16)
                copy = remote(to_z.at[n], from_z.at[n], zs.at[n], zr.at[n], at_mp(z_rows[i] * 4 + x))
                copy.start()
                z_sends.append(copy)
        for n, copy in enumerate(z_sends):
            copy.wait_recv()
            acc = acc + from_z[n].astype(F32)
        return acc, sends + z_sends

    loads[4].wait()
    summed, sends1 = reduce_scatter(
        attended, wo, part, part_x, part_z, sent_z, x_s, x_r, z_s, z_r, drain_attention
    )
    columns = pl.ds(pl.multiple_of(m * HEAD, HEAD), HEAD)
    residual = (hidden[:, columns].astype(F32) + summed).astype(BF16)

    gathered[m] = residual
    g_copies = []

    def share(block, dev):
        n = len(g_copies)
        copy = remote(gathered.at[block], gathered.at[block], g_s.at[n], g_r.at[block], dev)
        copy.start()
        g_copies.append(copy)

    def arrived(block):
        remote(
            gathered.at[block], gathered.at[block], g_s.at[0], g_r.at[block], z_peers[0]
        ).wait_recv()

    for i in (3, 2):
        share(m, at_mp(z_rows[i] * 4 + x))
    for dev in x_peers:
        share(m, dev)
    for hop in (2, 1, 3, 0):
        share(m, at_mp(z_rows[1] * 4 + lax.rem(x + hop, 4)))
    for i in (3, 2):
        arrived(z_rows[i] * 4 + x)
        for dev in x_peers:
            share(z_rows[i] * 4 + x, dev)
    arrived(z_rows[1] * 4 + x)
    for k in (5, 6, 7):
        loads[k].wait()
    square = jnp.zeros((TOK, HEAD), F32)
    gate, up = None, None
    for i in (0, 1, 3, 2):
        for hop in (1, 3, 2):
            arrived(z_rows[i] * 4 + lax.rem(x + hop, 4))
        base = z_rows[i] * 4
        scaled = []
        for k in range(4):
            v = gathered[base + k].astype(F32)
            square = square + v * v
            cols = pl.ds(pl.multiple_of((base + k) * HEAD, HEAD), HEAD)
            scaled.append((v * post_gain[:, cols]).astype(BF16))
        scaled = jnp.concatenate(scaled, axis=1)
        rows = pl.ds(pl.multiple_of(base * HEAD, 4 * HEAD), 4 * HEAD)
        gate_part, up_part = dot(scaled, wg[rows, :], 1, 0), dot(scaled, wu[rows, :], 1, 0)
        gate = gate_part if gate is None else gate + gate_part
        up = up_part if up is None else up + up_part
    scale = lax.rsqrt(jnp.sum(square, axis=-1, keepdims=True) * (1.0 / 2048) + EPSILON)
    gate, up = gate * scale, up * scale
    middle = (gate / (1.0 + jnp.exp(-gate)) * up).astype(BF16)

    def drain_residual():
        for copy in sends1 + g_copies:
            copy.wait_send()

    loads[8].wait()
    summed, sends2 = reduce_scatter(
        middle, wd, part2, part2_x, part2_z, sent2_z, x2_s, x2_r, z2_s, z2_r, drain_residual
    )
    out_ref[0] = (residual.astype(F32) + summed).astype(BF16)

    for copy in sends2:
        copy.wait_send()


def local(
    hidden_in,
    input_gain,
    w_query,
    key_value_weight,
    query_gain,
    key_gain,
    w_out,
    post_gain,
    w_gate,
    w_up,
    w_down,
    prefix_slot_cache,
    block_table,
    request_prefix,
    suffix_lengths,
):
    my_model = lax.axis_index("mp")
    cache = lax.dynamic_slice_in_dim(prefix_slot_cache, lax.div(my_model, 2), 1, 2).reshape(512, 2 * HEAD)

    def in_hbm(value):
        return pltpu.with_memory_space_constraint(value, pltpu.HBM)

    vmem = pl.BlockSpec(memory_space=pltpu.VMEM)
    smem = pl.BlockSpec(memory_space=pltpu.SMEM)
    hbm = pl.BlockSpec(memory_space=pl.ANY)
    V = pltpu.VMEM
    D = pltpu.SemaphoreType.DMA
    block = (TOK, HEAD)
    both = pl.pallas_call(
        kernel,
        out_shape=jax.ShapeDtypeStruct((2, TOK, HEAD), BF16),
        in_specs=[smem] * 3 + [hbm] * 3 + [vmem] * 3 + [hbm] * 6,
        out_specs=vmem,
        scratch_shapes=[
            V((128, 2048), BF16),
            V((1, 2048), F32),
            V((1, 2048), F32),
            V((2048, 128), BF16),
            V((2048, 256), BF16),
            V((128, 2048), BF16),
            V((2048, 384), BF16),
            V((2048, 384), BF16),
            V((384, 2048), BF16),
            V((128, 2048), BF16),
            V((4, 256, 128), BF16),
            V((4, 128, 256), BF16),
            V((8,) + block, BF16),
            V((3, 2) + block, BF16),
            V((2, 128, 512), F32),
            V((2, 8, 512), F32),
            V((8,) + block, BF16),
            V((8, 8, 128), F32),
            V((8,) + block, BF16),
            V((8, 8, 128), F32),
            V((8, 512), jnp.int32),
            V((4, 4) + block, BF16),
            V((4, 3) + block, BF16),
            V((3,) + block, BF16),
            V((3,) + block, BF16),
            V((4, 4) + block, BF16),
            V((4, 3) + block, BF16),
            V((3,) + block, BF16),
            V((3,) + block, BF16),
            V((16,) + block, BF16),
            D((9,)),
            D((2,)),
            D((2,)),
            D((2,)),
            D((2,)),
            D((2,)),
            D((2,)),
            D((7,)),
            D((8,)),
            D((8,)),
            D((8,)),
            D((8,)),
            D((8,)),
            D((4, 3)),
            D((4, 3)),
            D((3,)),
            D((3,)),
            D((4, 3)),
            D((4, 3)),
            D((3,)),
            D((3,)),
            D((15,)),
            D((16,)),
            pltpu.SemaphoreType.REGULAR,
        ],
        compiler_params=pltpu.CompilerParams(
            collective_id=0, has_side_effects=True, vmem_limit_bytes=48 * 1024 * 1024
        ),
        name="layer",
    )(
        block_table,
        request_prefix,
        suffix_lengths,
        in_hbm(hidden_in),
        in_hbm(input_gain.reshape(1, -1)),
        in_hbm(post_gain.reshape(1, -1)),
        query_gain.reshape(1, -1),
        key_gain.reshape(1, -1),
        cache,
        in_hbm(w_query),
        in_hbm(key_value_weight),
        in_hbm(w_out),
        in_hbm(w_gate),
        in_hbm(w_up),
        in_hbm(w_down),
    )

    return both[0], both[1]


def solution(mesh):
    in_specs = (
        P("seq", None),
        P(),
        P(None, "mp"),
        P(None, "mp"),
        P(),
        P(),
        P("mp", None),
        P(),
        P(None, "mp"),
        P(None, "mp"),
        P("mp", None),
        P("seq", None, None, None),
        P(),
        P(),
        P(),
    )
    out_specs = (P("seq", "mp"), P("seq", "mp"))
    return jax.shard_map(local, mesh=mesh, in_specs=in_specs, out_specs=out_specs, check_vma=False)
```
